32 devices in a mesh: groups: 2 (over y), tm: 4 (over z), lon: 2 (over x), probe: 2 (over core).
Axes of the slice: x: 2, y: 2, z: 4, core: 2. Of those that a mesh axis runs over, the one named last changes fastest.
Arguments:
- winds: bfloat16 [2, 8, 2, 36, 72, 192], P(None, ('groups', 'tm'), None, None, 'lon'), parts along dimension 1, may hold values from -0.44921875 to 0.44921875
- mixing: float32 [36, 36], replicated, as said below
- obs_cell: int32 [8, 2, 2048], P(('groups', 'tm'), 'lon'), parts along dimension 0, may hold values from 0 to 248831
- obs_weight: float32 [8, 2, 2048], P(('groups', 'tm'), 'lon'), parts along dimension 0, may hold values from 0.5 to 4
- probe_sign: int32 [4, 8, 2, 2048], P('probe', ('groups', 'tm'), 'lon'), parts along dimension 1, may hold values from 0 to 1
- week_map: int32 [8, 2], P(('groups', 'tm')), parts along dimension 0, may hold values from 0 to 1
- prior_precision: float32 [4, 72, 192], P('groups', 'lon', 'tm'), parts along dimension 0, may hold values from 0.1 to 1
Outputs:
- hessian_diag: float32 [2, 4, 72, 192], P('probe', 'groups', 'lon', 'tm'), parts along dimension 1
The draws below stay inside these ranges and needn't reach their ends.
There are 2 independent parts, one for each index of `groups`. The reference program is written for one: setup_inputs(seed, part) draws one part's arguments, and reference() takes and returns one part's arrays. A program takes and returns all parts, laid end to end along the dimension named above; an argument that names none is the same for every part. Nothing has to cross between parts.
Inputs may be any that keep to these rules, and one draw needn't show every extreme that they name: mixing = 0.55 on the diagonal plus 0.45 / 36 times a factor between 0.5 and 1.4 in every entry.
All inputs are finite; a program needn't handle non-finite values.
Results may differ from the reference program's by a relative error of at most 0.0003.
Values may be sent and summed in bfloat16 or wider, within the bound.
A program may use at most 128 MiB of HBM per device.

```python
import math
import jax
import jax.numpy as jnp
from jax import lax

LEV = 36
LAT = 192
LON_DEV = 36
HOURS = 2
PROBE_DEV = 2
OBS_DEV = 2048
WEEKS = 2
SECTIONS = 4
BANDS = 2
LONS = 72
PROBE_SETS = 2
PROBES = 4


def draw_mixing(key, part):
    spread = jax.random.uniform(key, (LEV, LEV), jnp.float32, 0.5, 1.4)
    diagonal = (jnp.arange(LEV)[:, None] == jnp.arange(LEV)[None, :]).astype(jnp.float32)
    return 0.55 * diagonal + 0.45 * spread / LEV


def plant(drawn, key, least, high):
    extent = drawn.shape
    index_at = [jax.random.randint(jax.random.fold_in(key, axis), (), 0, extent[axis]) for axis in range(len(extent))]
    drawn = drawn.at[tuple(index_at)].set(least)
    longest = extent.index(max(extent))
    index_at[longest] = (index_at[longest] + 1) % extent[longest]
    return drawn.at[tuple(index_at)].set(high)


def block_levels(key, extent, cuts, low, largest):
    gain = 1.0
    for axis_at, parts in cuts:
        steps = jax.random.uniform(jax.random.fold_in(jax.random.fold_in(key, 6), axis_at), (parts,), jnp.float32, low / len(cuts), largest / len(cuts))
        gain = gain * jnp.repeat(jnp.exp(steps), extent[axis_at] // parts).reshape((-1,) + (1,) * (len(extent) - 1 - axis_at))
    return gain


def setup_inputs(seed: int = 0, part: int = 0) -> dict:
    key_of = jax.random.split(jax.random.key(seed), 8)
    part_splits = jax.random.split(jax.random.fold_in(key_of[7], part), 8)
    return {
        "winds": jnp.clip(jax.random.uniform(part_splits[0], (2, SECTIONS, HOURS, LEV, LONS, LAT), jnp.float32, -0.44921875, 0.44921875) * block_levels(part_splits[0], (2, SECTIONS, HOURS, LEV, LONS, LAT), ((1, 4), (4, 2)), -0.4, 0.0), -0.44921875, 0.44921875).astype(jnp.bfloat16),
        "mixing": draw_mixing(jax.random.fold_in(key_of[7], 71), part),
        "obs_cell": plant(jax.random.randint(part_splits[2], (SECTIONS, BANDS, OBS_DEV), 0, LEV * LON_DEV * LAT), jax.random.fold_in(part_splits[2], 1), 0, (LEV * LON_DEV * LAT) - 1).astype(jnp.int32),
        "obs_weight": jnp.clip(jnp.exp(math.log(4.0) - 2.0794415 * jax.random.uniform(part_splits[3], (SECTIONS, BANDS, OBS_DEV), jnp.float32) ** block_levels(part_splits[3], (SECTIONS, BANDS, OBS_DEV), ((0, 4), (1, 2)), -0.2, 0.2)), 0.5, 4.0),
        "probe_sign": plant(jax.random.randint(part_splits[4], (PROBES, SECTIONS, BANDS, OBS_DEV), 0, 2), jax.random.fold_in(part_splits[4], 1), 0, 1).astype(jnp.int32),
        "week_map": plant(jax.random.randint(part_splits[5], (SECTIONS, HOURS), 0, WEEKS), jax.random.fold_in(part_splits[5], 1), 0, WEEKS - 1).astype(jnp.int32),
        "prior_precision": jnp.clip(jnp.exp(math.log(1.0) - 2.3025851 * jax.random.uniform(part_splits[6], (WEEKS, LONS, LAT), jnp.float32) ** block_levels(part_splits[6], (WEEKS, LONS, LAT), ((1, 2), (2, 4)), -0.2, 0.2)), 0.1, 1.0),
    }


def adjoint_step(adjoint, east_face, north_face, mixing):
    adjoint = jnp.einsum('lk,...lxy->...kxy', mixing, adjoint, precision=lax.Precision.HIGHEST)
    east_pos = jnp.maximum(east_face, 0.0)
    west_neg = jnp.minimum(jnp.roll(east_face, 1, axis=-2), 0.0)
    adjoint = adjoint + east_pos * (jnp.roll(adjoint, -1, axis=-2) - adjoint) + west_neg * (adjoint - jnp.roll(adjoint, 1, axis=-2))
    lat_count = north_face.shape[-1]
    row_keep = (jnp.arange(lat_count) < lat_count - 1).astype(north_face.dtype)
    north_cut = north_face * row_keep
    north_pos = jnp.maximum(north_cut, 0.0)
    south_neg = jnp.minimum(jnp.concatenate([jnp.zeros_like(north_cut[..., :1]), north_cut[..., :-1]], axis=-1), 0.0)
    above_row = jnp.concatenate([adjoint[..., 1:], jnp.zeros_like(adjoint[..., :1])], axis=-1)
    below_row = jnp.concatenate([jnp.zeros_like(adjoint[..., :1]), adjoint[..., :-1]], axis=-1)
    return adjoint + north_pos * (above_row - adjoint) + south_neg * (adjoint - below_row)


def reference(winds, mixing, obs_cell, obs_weight, probe_sign, week_map, prior_precision):
    sign_vals = (2 * probe_sign - 1).astype(jnp.float32)
    value = sign_vals * obs_weight[None]
    level_id = obs_cell // (LON_DEV * LAT)
    remainder = obs_cell % (LON_DEV * LAT)
    column = remainder // LAT
    lat_id = remainder % LAT
    global_col = column + (jnp.arange(BANDS, dtype=jnp.int32) * LON_DEV)[None, :, None]
    flat_index = ((level_id * LONS + global_col) * LAT + lat_id).astype(jnp.int32)
    hour_count = SECTIONS * HOURS

    def per_hour(state_pair, step_id):
        adjoint, flux_adj = state_pair
        section_id = step_id // HOURS
        hour_id = step_id % HOURS
        places = lax.dynamic_index_in_dim(flat_index, section_id, 0, keepdims=False).reshape(-1)
        hour_gate = (hour_id == 0).astype(jnp.float32)
        injected = lax.dynamic_index_in_dim(value, section_id, 1, keepdims=False) * hour_gate
        adjoint = adjoint.reshape(PROBES, -1).at[:, places].add(injected.reshape(PROBES, -1)).reshape(PROBES, LEV, LONS, LAT)
        week_id = week_map[section_id, hour_id]
        onehot = (jnp.arange(WEEKS) == week_id).astype(jnp.float32)
        flux_adj = flux_adj + onehot[None, :, None, None] * adjoint[:, None, 0]
        east_face = winds[0, section_id, hour_id].astype(jnp.float32)
        north_face = winds[1, section_id, hour_id].astype(jnp.float32)
        adjoint = adjoint_step(adjoint, east_face, north_face, mixing)
        return (adjoint, flux_adj), None

    start = (jnp.zeros((PROBES, LEV, LONS, LAT), jnp.float32), jnp.zeros((PROBES, WEEKS, LONS, LAT), jnp.float32))
    (adjoint, flux_adj), unused = lax.scan(per_hour, start, jnp.arange(hour_count - 1, -1, -1, dtype=jnp.int32))
    squares = (flux_adj * flux_adj).reshape(PROBE_SETS, PROBE_DEV, WEEKS, LONS, LAT)
    return prior_precision[None] + jnp.mean(squares, axis=1)
```

```python
import functools

import jax
import jax.numpy as jnp
from jax import lax
from jax.experimental import pallas as pl
from jax.experimental.pallas import tpu as pltpu
from jax.sharding import PartitionSpec as P


def split2(x):
    high = x.astype(jnp.bfloat16)
    low = (x - high.astype(jnp.float32)).astype(jnp.bfloat16)
    return high, low


def sweep_kernel(dims, weeks_ref, mix_ref, low_ref, own_ref, high_ref, obs_ref, out_ref, state, mixed, flux, wind):
    hours, hours_sec, halo, band_cols, lev, lev_pad, lat_rows, own, left, window, probes = dims
    ext_cols = band_cols + 2 * halo
    lanes = window * probes
    step = pl.program_id(0)
    hour = hours - 1 - step
    first_row = lax.axis_index("tm") * own - left

    @pl.when(step == 0)
    def _():
        state[...] = jnp.zeros_like(state)
        mixed[...] = jnp.zeros_like(mixed)
        flux[...] = jnp.zeros_like(flux)

    @pl.when(lax.rem(hour, hours_sec) == 0)
    def _():
        cols_at = 4
        count = obs_ref.shape[-1]
        for piece, (begin, width, shift) in enumerate(
            ((halo, band_cols, 0), (0, halo, -band_cols), (halo + band_cols, halo, band_cols))
        ):
            cell = obs_ref[0, piece, 0:1, :].astype(jnp.int32)
            level = cell // (band_cols * lat_rows)
            rest = cell - level * (band_cols * lat_rows)
            column = rest // lat_rows
            row = rest - column * lat_rows - first_row
            place = (column + halo + shift - begin) * lev_pad + level
            sub = lax.broadcasted_iota(jnp.int32, (window, count), 0)
            hit = sub == row
            parts = [
                split2(jnp.where(hit, obs_ref[0, piece, 1 + p : 2 + p, :], 0.0))
                for p in range(probes)
            ]
            rhs = jnp.concatenate([x[0] for x in parts] + [x[1] for x in parts], axis=0)
            chunk = lax.broadcasted_iota(jnp.int32, (cols_at * lev_pad, count), 0)

            def body(i, carry):
                hot = (chunk == place - i * (cols_at * lev_pad)).astype(jnp.float32)
                got = lax.dot_general(
                    hot.astype(jnp.bfloat16), rhs, (((1,), (1,)), ((), ())),
                    preferred_element_type=jnp.float32,
                )
                add = got[:, :lanes] + got[:, lanes:]
                for c in range(cols_at):
                    at = begin + i * cols_at + c
                    state[at] += add[c * lev_pad : (c + 1) * lev_pad]
                return carry

            lax.fori_loop(0, width // cols_at, body, 0)

    week = weeks_ref[hour]
    flux[week] += state[halo : halo + band_cols, 0, :]

    wind[:halo] = low_ref[0]
    wind[halo : halo + band_cols] = own_ref[0]
    wind[halo + band_cols :] = high_ref[0]
    mix = mix_ref[...]

    def mixing(i, carry):
        x = jnp.concatenate([state[2 * i], state[2 * i + 1]], axis=1)
        low = x - x.astype(jnp.bfloat16).astype(jnp.float32)
        stack = jnp.concatenate([x, x, low], axis=0).astype(jnp.bfloat16)
        got = jnp.dot(mix, stack, preferred_element_type=jnp.float32)
        mixed[2 * i] = got[:, :lanes]
        mixed[2 * i + 1] = got[:, lanes:]
        return carry

    lax.fori_loop(0, ext_cols // 2, mixing, 0, unroll=4)

    lane = lax.broadcasted_iota(jnp.int32, (lev_pad, lanes), 1)
    first = lane < window
    grid_row = lax.rem(lane, window) + first_row
    keep = jnp.logical_and(grid_row >= 0, grid_row < lat_rows - 1)

    def advect(j, carry):
        packed = wind[j].astype(jnp.float32)
        turned = pltpu.roll(packed, window, 1)
        before = wind[j - 1].astype(jnp.float32)
        east = jnp.where(first, packed, turned)
        west = jnp.where(first, before, pltpu.roll(before, window, 1))
        north = jnp.where(first, turned, packed)
        north = jnp.where(keep, north, 0.0)
        south = pltpu.roll(north, 1, 1)
        here = mixed[j]
        g = (
            here
            + jnp.maximum(east, 0.0) * (mixed[j + 1] - here)
            + jnp.minimum(west, 0.0) * (here - mixed[j - 1])
        )
        above = pltpu.roll(g, lanes - 1, 1)
        below = pltpu.roll(g, 1, 1)
        state[j] = g + jnp.maximum(north, 0.0) * (above - g) + jnp.minimum(south, 0.0) * (g - below)
        return carry

    lax.fori_loop(1, ext_cols - 1, advect, 0, unroll=2)

    @pl.when(step == hours - 1)
    def _():
        square = flux[...] * flux[...]
        rolled = [
            square[w] + pltpu.roll(square[w], lanes - window, 1) for w in range(square.shape[0])
        ]
        for w in range(square.shape[0]):
            out_ref[w] = rolled[w] * 0.5


def on_device(winds, mixing, obs_cell, obs_weight, probe_sign, week_map, prior_precision):
    hours_sec = winds.shape[2]
    levels = winds.shape[3]
    band_cols = winds.shape[4]
    lat_rows = winds.shape[5]
    probes = probe_sign.shape[0]
    week_count, _, own = prior_precision.shape
    sections = lax.axis_size("tm")
    bands = lax.axis_size("lon")
    hours = sections * hours_sec
    lev_pad = -(-levels // 8) * 8
    halo = -(-hours // 4) * 4
    left = hours
    window = -(-(own + 2 * hours) // 64) * 64
    lanes = window * probes

    w = winds[:, 0].transpose(1, 3, 2, 0, 4)
    w = jnp.pad(w, ((0, 0), (0, 0), (0, lev_pad - levels), (0, 0), (left, window - own - left)))
    w = jnp.stack([w[..., d * own : d * own + window] for d in range(sections)])
    w = w.reshape(sections, hours_sec, band_cols, lev_pad, 2 * window)
    w = lax.all_to_all(w, "tm", 0, 0, tiled=True)
    w = w.reshape(hours, band_cols, lev_pad, 2 * window)
    right_way = [(i, (i + 1) % bands) for i in range(bands)]
    left_way = [(b, a) for a, b in right_way]
    low = lax.ppermute(w[:, band_cols - halo :], "lon", right_way)
    high = lax.ppermute(w[:, :halo], "lon", left_way)

    value = (2 * probe_sign[:, 0, 0] - 1).astype(jnp.float32) * obs_weight[0, 0][None]
    bundle = jnp.concatenate([obs_cell[0, 0].astype(jnp.float32)[None], value], axis=0)
    bundle = lax.all_gather(bundle, "tm")
    from_low = lax.ppermute(bundle, "lon", right_way)
    from_high = from_low if bands == 2 else lax.ppermute(bundle, "lon", left_way)
    obs = jnp.stack([bundle, from_low, from_high], axis=1)
    weeks = lax.all_gather(week_map[0], "tm").reshape(hours)

    mix = jnp.pad(mixing.T, ((0, lev_pad - levels),) * 2)
    high_mix = lax.reduce_precision(mix, 8, 7)
    mix = jnp.concatenate([high_mix, mix - high_mix, high_mix], axis=1).astype(jnp.bfloat16)

    dims = (
        hours, hours_sec, halo, band_cols, levels, lev_pad, lat_rows, own, left, window, probes
    )
    ext_cols = band_cols + 2 * halo
    estimate = pl.pallas_call(
        functools.partial(sweep_kernel, dims),
        out_shape=jax.ShapeDtypeStruct((week_count, band_cols, lanes), jnp.float32),
        grid_spec=pltpu.PrefetchScalarGridSpec(
            num_scalar_prefetch=1,
            grid=(hours,),
            in_specs=[
                pl.BlockSpec(mix.shape, lambda i, wk: (0, 0)),
                *(
                    pl.BlockSpec((1,) + x.shape[1:], lambda i, wk: (hours - 1 - i, 0, 0, 0))
                    for x in (low, w, high)
                ),
                pl.BlockSpec(
                    (1,) + obs.shape[1:], lambda i, wk: ((hours - 1 - i) // hours_sec, 0, 0, 0)
                ),
            ],
            out_specs=pl.BlockSpec((week_count, band_cols, lanes), lambda i, wk: (0, 0, 0)),
            scratch_shapes=[
                pltpu.VMEM((ext_cols, lev_pad, lanes), jnp.float32),
                pltpu.VMEM((ext_cols, lev_pad, lanes), jnp.float32),
                pltpu.VMEM((week_count, band_cols, lanes), jnp.float32),
                pltpu.VMEM((ext_cols, lev_pad, 2 * window), jnp.bfloat16),
            ],
        ),
        compiler_params=pltpu.CompilerParams(vmem_limit_bytes=48 << 20),
    )(weeks, mix, low, w, high, obs)
    return (prior_precision + estimate[..., left : left + own])[None]


def solution(mesh):
    placed = (
        P(None, ("groups", "tm"), None, None, "lon", None),
        P(),
        P(("groups", "tm"), "lon", None),
        P(("groups", "tm"), "lon", None),
        P("probe", ("groups", "tm"), "lon", None),
        P(("groups", "tm"), None),
        P("groups", "lon", "tm"),
    )
    return jax.shard_map(
        on_device,
        mesh=mesh,
        in_specs=placed,
        out_specs=P("probe", "groups", "lon", "tm"),
        check_vma=False,
    )
```

```python
import functools

import jax
import jax.numpy as jnp
from jax import lax
from jax.experimental import pallas as pl
from jax.experimental.pallas import tpu as pltpu
from jax.sharding import PartitionSpec as P


def split2(x):
    high = x.astype(jnp.bfloat16)
    low = (x - high.astype(jnp.float32)).astype(jnp.bfloat16)
    return high, low


def sweep_kernel(dims, weeks_ref, mix_ref, winds_ref, obs_ref, out_ref, state, mixed, flux):
    hours, hours_sec, halo, band_cols, lev, lev_pad, lat_rows, own, left, window, probes = dims
    ext_cols = band_cols + 2 * halo
    lanes = window * probes
    step = pl.program_id(0)
    hour = hours - 1 - step
    first_row = lax.axis_index("tm") * own - left

    @pl.when(step == 0)
    def _():
        state[...] = jnp.zeros_like(state)
        mixed[...] = jnp.zeros_like(mixed)
        flux[...] = jnp.zeros_like(flux)

    @pl.when(lax.rem(hour, hours_sec) == 0)
    def _():
        cols_at = 4
        count = obs_ref.shape[-1]
        for piece, (begin, width, shift) in enumerate(
            ((halo, band_cols, 0), (0, halo, -band_cols), (halo + band_cols, halo, band_cols))
        ):
            cell = obs_ref[0, piece, 0:1, :].astype(jnp.int32)
            level = cell // (band_cols * lat_rows)
            rest = cell - level * (band_cols * lat_rows)
            column = rest // lat_rows
            row = rest - column * lat_rows - first_row
            place = (column + halo + shift - begin) * lev_pad + level
            sub = lax.broadcasted_iota(jnp.int32, (window, count), 0)
            hit = sub == row
            parts = [
                split2(jnp.where(hit, obs_ref[0, piece, 1 + p : 2 + p, :], 0.0))
                for p in range(probes)
            ]
            rhs = jnp.concatenate([x[0] for x in parts] + [x[1] for x in parts], axis=0)
            chunk = lax.broadcasted_iota(jnp.int32, (cols_at * lev_pad, count), 0)

            def body(i, carry):
                hot = (chunk == place - i * (cols_at * lev_pad)).astype(jnp.float32)
                got = lax.dot_general(
                    hot.astype(jnp.bfloat16), rhs, (((1,), (1,)), ((), ())),
                    preferred_element_type=jnp.float32,
                )
                add = got[:, :lanes] + got[:, lanes:]
                for c in range(cols_at):
                    at = begin + i * cols_at + c
                    state[at] += add[c * lev_pad : (c + 1) * lev_pad]
                return carry

            lax.fori_loop(0, width // cols_at, body, 0)

    week = weeks_ref[hour]
    flux[week] += state[halo : halo + band_cols, 0, :]

    @pl.when(hour > 0)
    def _():
        mix = mix_ref[...]

        def mixing(i, carry):
            x = jnp.concatenate([state[2 * i], state[2 * i + 1]], axis=1)
            low = x - x.astype(jnp.bfloat16).astype(jnp.float32)
            stack = jnp.concatenate([x, x, low], axis=0).astype(jnp.bfloat16)
            got = jnp.dot(mix, stack, preferred_element_type=jnp.float32)
            mixed[2 * i] = got[:, :lanes]
            mixed[2 * i + 1] = got[:, lanes:]
            return carry

        lax.fori_loop(0, ext_cols // 2, mixing, 0, unroll=4)

        lane = lax.broadcasted_iota(jnp.int32, (lev_pad, lanes), 1)
        first = lane < window
        grid_row = lax.rem(lane, window) + first_row
        keep = jnp.logical_and(grid_row >= 0, grid_row < lat_rows - 1)

        def advect(j, carry):
            packed = winds_ref[0, j].astype(jnp.float32)
            turned = pltpu.roll(packed, window, 1)
            before = winds_ref[0, j - 1].astype(jnp.float32)
            east = jnp.where(first, packed, turned)
            west = jnp.where(first, before, pltpu.roll(before, window, 1))
            north = jnp.where(first, turned, packed)
            north = jnp.where(keep, north, 0.0)
            south = pltpu.roll(north, 1, 1)
            here = mixed[j]
            g = (
                here
                + jnp.maximum(east, 0.0) * (mixed[j + 1] - here)
                + jnp.minimum(west, 0.0) * (here - mixed[j - 1])
            )
            above = pltpu.roll(g, lanes - 1, 1)
            below = pltpu.roll(g, 1, 1)
            state[j] = g + jnp.maximum(north, 0.0) * (above - g) + jnp.minimum(south, 0.0) * (g - below)
            return carry

        lax.fori_loop(1, ext_cols - 1, advect, 0, unroll=2)

    @pl.when(step == hours - 1)
    def _():
        square = flux[...] * flux[...]
        rolled = [
            square[w] + pltpu.roll(square[w], lanes - window, 1) for w in range(square.shape[0])
        ]
        for w in range(square.shape[0]):
            out_ref[w] = rolled[w] * 0.5


def window_kernel(dims, winds_ref, out_ref, *tmp):
    lev, lev_pad, cols, lat, own, left, window = dims
    d = pl.program_id(1)
    wide = -(-lat // 128) * 128
    shift = lax.rem(left - d * own + 2 * wide, wide)
    row = lax.broadcasted_iota(jnp.int32, (cols, wide), 1)
    fill = jnp.zeros((cols, wide - lat), jnp.float32)

    for part in tmp:
        part[...] = jnp.zeros_like(part)

    def level(i, carry):
        moved = []
        for comp in range(2):
            x = jnp.concatenate([winds_ref[comp, 0, 0, i].astype(jnp.float32), fill], axis=1)
            at = row - comp * window
            at_row = at + d * own - left
            inside = (at >= 0) & (at < window) & (at_row >= 0) & (at_row < lat)
            turn = shift + comp * window
            turn = jnp.where(turn >= wide, turn - wide, turn)
            moved.append(jnp.where(inside, pltpu.roll(x, turn, 1), 0.0))
        both = moved[0] + moved[1]
        for n, part in enumerate(tmp):
            part[pl.ds(i, cols, stride=lev_pad), :] = both[:, n * 128 : (n + 1) * 128]
        return carry

    lax.fori_loop(0, lev, level, 0, unroll=2)

    def column(c, carry):
        for n, part in enumerate(tmp):
            block = part[pl.ds(pl.multiple_of(c * lev_pad, 8), lev_pad), :]
            out_ref[0, 0, c, :, n * 128 : (n + 1) * 128] = block.astype(jnp.bfloat16)
        return carry

    lax.fori_loop(0, cols, column, 0, unroll=4)


def spread_kernel(dims, pack, bundle, winds, obs, zs, zr, xs, xr, hs, hr, gs, gr, os, orr, local):
    sections, bands, cols, halo = dims
    me = lax.axis_index("tm")
    band = lax.axis_index("lon")
    core = lax.axis_index("probe")
    half = cols // 2
    sides = (band, lax.rem(band + 1, bands), lax.rem(band + bands - 1, bands))

    def remote(src, dst, send, recv, tm, lon, probe):
        copy = pltpu.make_async_remote_copy(
            src_ref=src, dst_ref=dst, send_sem=send, recv_sem=recv,
            device_id={"tm": tm, "lon": lon, "probe": probe},
            device_id_type=pl.DeviceIdType.MESH,
        )
        copy.start()
        return copy

    barrier = pltpu.get_barrier_semaphore()
    for k in range(sections):
        tm = lax.rem(me + k, sections)
        for n, lon in enumerate(sides):
            if k or n:
                pl.semaphore_signal(
                    barrier, inc=1, device_id={"tm": tm, "lon": lon, "probe": core},
                    device_id_type=pl.DeviceIdType.MESH,
                )
    pl.semaphore_signal(
        barrier, inc=1, device_id={"tm": me, "lon": band, "probe": 1 - core},
        device_id_type=pl.DeviceIdType.MESH,
    )
    own_winds = pltpu.make_async_copy(pack.at[me], winds.at[me, :, pl.ds(halo, cols)], local.at[0])
    own_winds.start()
    own_obs = pltpu.make_async_copy(bundle, obs.at[me, 0], local.at[1])
    own_obs.start()
    pl.semaphore_wait(barrier, 3 * sections)

    mine = pl.ds(halo + half * core, half)
    edge = pl.ds((1 - core) * (halo + cols), halo)
    beside = lax.rem(band + bands + 2 * core - 1, bands)
    z_copies, x_copies, h_copies, g_copies, o_copies = [], [], [], [], []
    for k in range(1, sections):
        tm = lax.rem(me + k, sections)
        z_copies.append(
            remote(
                pack.at[tm, :, pl.ds(half * core, half)], winds.at[me, :, mine],
                zs.at[k], zr.at[k], tm, band, core,
            )
        )
    for k in range(sections):
        tm = lax.rem(me + k, sections)
        for n, lon in enumerate(sides):
            if k or n:
                o_copies.append(
                    remote(
                        bundle, obs.at[me, n], os.at[3 * k + n], orr.at[3 * k + n], tm, lon, core
                    )
                )
    x_copies.append(
        remote(
            pack.at[me, :, pl.ds(core * (cols - halo), halo)], winds.at[me, :, edge],
            xs.at[0], xr.at[0], me, beside, core,
        )
    )
    for k in range(1, sections):
        source = lax.rem(me + sections - k, sections)
        z_copies[k - 1].wait_recv()
        h_copies.append(
            remote(
                winds.at[source, :, mine], winds.at[source, :, mine],
                hs.at[k], hr.at[k], me, band, 1 - core,
            )
        )
        if halo > half:
            h_copies[-1].wait_recv()
        x_copies.append(
            remote(
                winds.at[source, :, pl.ds(halo + core * (cols - halo), halo)],
                winds.at[source, :, edge], xs.at[k], xr.at[k], me, beside, core,
            )
        )
    for k in range(sections):
        source = lax.rem(me + sections - k, sections)
        x_copies[k].wait_recv()
        g_copies.append(
            remote(
                winds.at[source, :, edge], winds.at[source, :, edge],
                gs.at[k], gr.at[k], me, band, 1 - core,
            )
        )
    if halo <= half:
        for copy in h_copies:
            copy.wait_recv()
    for copy in g_copies + o_copies:
        copy.wait_recv()
    for copy in z_copies + x_copies + h_copies + g_copies + o_copies:
        copy.wait_send()
    own_winds.wait()
    own_obs.wait()


def on_device(winds, mixing, obs_cell, obs_weight, probe_sign, week_map, prior_precision):
    hours_sec = winds.shape[2]
    levels = winds.shape[3]
    band_cols = winds.shape[4]
    lat_rows = winds.shape[5]
    probes = probe_sign.shape[0]
    week_count, _, own = prior_precision.shape
    sections = lax.axis_size("tm")
    bands = lax.axis_size("lon")
    hours = sections * hours_sec
    lev_pad = -(-levels // 8) * 8
    halo = -(-hours // 4) * 4
    left = hours
    window = -(-(own + 2 * hours) // 64) * 64
    lanes = window * probes

    shape = (hours_sec, sections, band_cols, lev_pad, 2 * window)
    pack = pl.pallas_call(
        functools.partial(
            window_kernel, (levels, lev_pad, band_cols, lat_rows, own, left, window)
        ),
        out_shape=jax.ShapeDtypeStruct((sections, hours_sec) + shape[2:], jnp.bfloat16),
        grid=(hours_sec, sections),
        in_specs=[
            pl.BlockSpec(
                (2, 1, 1, levels, band_cols, lat_rows), lambda h, d: (0, 0, h, 0, 0, 0)
            )
        ],
        out_specs=pl.BlockSpec((1, 1) + shape[2:], lambda h, d: (d, h, 0, 0, 0)),
        scratch_shapes=[pltpu.VMEM((band_cols * lev_pad, 128), jnp.float32)]
        * (2 * window // 128),
        compiler_params=pltpu.CompilerParams(vmem_limit_bytes=40 << 20),
    )(winds)

    value = (2 * probe_sign[:, 0, 0] - 1).astype(jnp.float32) * obs_weight[0, 0][None]
    count = value.shape[1]
    week_row = jnp.pad(week_map.astype(jnp.float32), ((0, 0), (0, count - hours_sec)))
    bundle = jnp.concatenate([obs_cell[0].astype(jnp.float32), value, week_row], axis=0)
    ext_cols = band_cols + 2 * halo
    sem = pltpu.SemaphoreType.DMA
    w, obs = pl.pallas_call(
        functools.partial(spread_kernel, (sections, bands, band_cols, halo)),
        out_shape=(
            jax.ShapeDtypeStruct(
                (sections, hours_sec, ext_cols, lev_pad, 2 * window), jnp.bfloat16
            ),
            jax.ShapeDtypeStruct((sections, 3) + bundle.shape, jnp.float32),
        ),
        in_specs=[pl.BlockSpec(memory_space=pl.ANY)] * 2,
        out_specs=(pl.BlockSpec(memory_space=pl.ANY),) * 2,
        scratch_shapes=[sem((sections,))] * 8 + [sem((3 * sections,))] * 2 + [sem((2,))],
        compiler_params=pltpu.CompilerParams(collective_id=0, has_side_effects=True),
    )(pack, bundle)
    w = w.reshape((hours,) + w.shape[2:])
    weeks = obs[:, 0, 1 + probes, :hours_sec].astype(jnp.int32).reshape(hours)

    mix = jnp.pad(mixing.T, ((0, lev_pad - levels),) * 2)
    high_mix = lax.reduce_precision(mix, 8, 7)
    mix = jnp.concatenate([high_mix, mix - high_mix, high_mix], axis=1).astype(jnp.bfloat16)

    dims = (
        hours, hours_sec, halo, band_cols, levels, lev_pad, lat_rows, own, left, window, probes
    )
    estimate = pl.pallas_call(
        functools.partial(sweep_kernel, dims),
        out_shape=jax.ShapeDtypeStruct((week_count, band_cols, lanes), jnp.float32),
        grid_spec=pltpu.PrefetchScalarGridSpec(
            num_scalar_prefetch=1,
            grid=(hours,),
            in_specs=[
                pl.BlockSpec(mix.shape, lambda i, wk: (0, 0)),
                pl.BlockSpec((1,) + w.shape[1:], lambda i, wk: (hours - 1 - i, 0, 0, 0)),
                pl.BlockSpec(
                    (1,) + obs.shape[1:], lambda i, wk: ((hours - 1 - i) // hours_sec, 0, 0, 0)
                ),
            ],
            out_specs=pl.BlockSpec((week_count, band_cols, lanes), lambda i, wk: (0, 0, 0)),
            scratch_shapes=[
                pltpu.VMEM((ext_cols, lev_pad, lanes), jnp.float32),
                pltpu.VMEM((ext_cols, lev_pad, lanes), jnp.float32),
                pltpu.VMEM((week_count, band_cols, lanes), jnp.float32),
            ],
        ),
        compiler_params=pltpu.CompilerParams(vmem_limit_bytes=48 << 20),
    )(weeks, mix, w, obs)
    return (prior_precision + estimate[..., left : left + own])[None]


def solution(mesh):
    placed = (
        P(None, ("groups", "tm"), None, None, "lon", None),
        P(),
        P(("groups", "tm"), "lon", None),
        P(("groups", "tm"), "lon", None),
        P("probe", ("groups", "tm"), "lon", None),
        P(("groups", "tm"), None),
        P("groups", "lon", "tm"),
    )
    return jax.shard_map(
        on_device,
        mesh=mesh,
        in_specs=placed,
        out_specs=P("probe", "groups", "lon", "tm"),
        check_vma=False,
    )
```

```python
import functools

import jax
import jax.numpy as jnp
from jax import lax
from jax.experimental import pallas as pl
from jax.experimental.pallas import tpu as pltpu
from jax.sharding import PartitionSpec as P


def split2(x):
    high = x.astype(jnp.bfloat16)
    low = (x - high.astype(jnp.float32)).astype(jnp.bfloat16)
    return high, low


def sweep_kernel(dims, weeks_ref, mix_ref, winds_ref, obs_ref, out_ref, state, mixed, flux):
    hours, hours_sec, halo, band_cols, lev, lev_pad, lat_rows, own, left, window, probes = dims
    ext_cols = band_cols + 2 * halo
    lanes = window * probes
    step = pl.program_id(0)
    hour = hours - 1 - step
    first_row = lax.axis_index("tm") * own - left

    @pl.when(step == 0)
    def _():
        state[...] = jnp.zeros_like(state)
        mixed[...] = jnp.zeros_like(mixed)
        flux[...] = jnp.zeros_like(flux)

    @pl.when(lax.rem(hour, hours_sec) == 0)
    def _():
        count = obs_ref.shape[-1]
        for piece, (begin, width, shift) in enumerate(
            ((halo, band_cols, 0), (0, halo, -band_cols), (halo + band_cols, halo, band_cols))
        ):
            cell = obs_ref[0, piece, 0:1, :].astype(jnp.int32)
            level = cell // (band_cols * lat_rows)
            rest = cell - level * (band_cols * lat_rows)
            column = rest // lat_rows
            row = rest - column * lat_rows - first_row
            place = (column + halo + shift - begin) * lev_pad + level
            sub = lax.broadcasted_iota(jnp.int32, (window, count), 0)
            hit = sub == row
            parts = [
                split2(jnp.where(hit, obs_ref[0, piece, 1 + p : 2 + p, :], 0.0))
                for p in range(probes)
            ]
            rhs = jnp.concatenate([x[0] for x in parts] + [x[1] for x in parts], axis=0)
            cols_at = max(n for n in range(1, 19) if width % n == 0)
            chunk = lax.broadcasted_iota(jnp.int32, (cols_at * lev_pad, count), 0)

            def body(i, carry):
                hot = (chunk == place - i * (cols_at * lev_pad)).astype(jnp.float32)
                got = lax.dot_general(
                    hot.astype(jnp.bfloat16), rhs, (((1,), (1,)), ((), ())),
                    preferred_element_type=jnp.float32,
                )
                add = got[:, :lanes] + got[:, lanes:]
                for c in range(cols_at):
                    at = begin + i * cols_at + c
                    state[at] += add[c * lev_pad : (c + 1) * lev_pad]
                return carry

            lax.fori_loop(0, width // cols_at, body, 0)

    week = weeks_ref[hour]
    flux[week] += state[halo : halo + band_cols, 0, :]

    @pl.when(hour > 0)
    def _():
        mix = mix_ref[...]
        wide = 8
        deep = 4

        def mixing(i, carry):
            at = jnp.minimum(halo - hour + i * wide, ext_cols - wide)
            for c in range(0, wide, 2):
                x = jnp.concatenate([state[at + c], state[at + c + 1]], axis=1)
                low = x - x.astype(jnp.bfloat16).astype(jnp.float32)
                stack = jnp.concatenate([x, x, low], axis=0).astype(jnp.bfloat16)
                got = jnp.dot(mix, stack, preferred_element_type=jnp.float32)
                mixed[at + c] = got[:, :lanes]
                mixed[at + c + 1] = got[:, lanes:]
            return carry

        lax.fori_loop(0, (band_cols + 2 * hour + wide - 1) // wide, mixing, 0)

        lane = lax.broadcasted_iota(jnp.int32, (lev_pad, lanes), 1)
        first = lane < window
        grid_row = lax.rem(lane, window) + first_row
        keep = jnp.logical_and(grid_row >= 0, grid_row < lat_rows - 1)

        def advect(i, carry):
            at = jnp.minimum(halo - hour + 1 + i * deep, ext_cols - 1 - deep)
            packed = winds_ref[0, at - 1].astype(jnp.float32)
            west = jnp.where(first, packed, pltpu.roll(packed, window, 1))
            before, here = mixed[at - 1], mixed[at]
            for c in range(deep):
                after = mixed[at + c + 1]
                packed = winds_ref[0, at + c].astype(jnp.float32)
                turned = pltpu.roll(packed, window, 1)
                east = jnp.where(first, packed, turned)
                north = jnp.where(keep, jnp.where(first, turned, packed), 0.0)
                south = pltpu.roll(north, 1, 1)
                g = (
                    here
                    + jnp.maximum(east, 0.0) * (after - here)
                    + jnp.minimum(west, 0.0) * (here - before)
                )
                above = pltpu.roll(g, lanes - 1, 1)
                below = pltpu.roll(g, 1, 1)
                state[at + c] = (
                    g + jnp.maximum(north, 0.0) * (above - g) + jnp.minimum(south, 0.0) * (g - below)
                )
                before, here, west = here, after, east
            return carry

        lax.fori_loop(0, (band_cols + 2 * hour - 2 + deep - 1) // deep, advect, 0)

    @pl.when(step == hours - 1)
    def _():
        square = flux[...] * flux[...]
        rolled = [
            square[w] + pltpu.roll(square[w], lanes - window, 1) for w in range(square.shape[0])
        ]
        for w in range(square.shape[0]):
            out_ref[w] = rolled[w] * 0.5


def window_kernel(dims, winds_ref, out_ref, *tmp):
    lev, lev_pad, cols, lat, own, left, window = dims
    d = pl.program_id(1)
    wide = -(-lat // 128) * 128
    shift = lax.rem(left - d * own + 2 * wide, wide)
    row = lax.broadcasted_iota(jnp.int32, (cols, wide), 1)
    fill = jnp.zeros((cols, wide - lat), jnp.float32)

    for part in tmp:
        part[...] = jnp.zeros_like(part)

    def level(i, carry):
        moved = []
        for comp in range(2):
            x = jnp.concatenate([winds_ref[comp, 0, 0, i].astype(jnp.float32), fill], axis=1)
            at = row - comp * window
            at_row = at + d * own - left
            inside = (at >= 0) & (at < window) & (at_row >= 0) & (at_row < lat)
            turn = shift + comp * window
            turn = jnp.where(turn >= wide, turn - wide, turn)
            moved.append(jnp.where(inside, pltpu.roll(x, turn, 1), 0.0))
        both = moved[0] + moved[1]
        for n, part in enumerate(tmp):
            part[pl.ds(i, cols, stride=lev_pad), :] = both[:, n * 128 : (n + 1) * 128]
        return carry

    lax.fori_loop(0, lev, level, 0, unroll=2)

    def column(c, carry):
        for n, part in enumerate(tmp):
            block = part[pl.ds(pl.multiple_of(c * lev_pad, 8), lev_pad), :]
            out_ref[0, 0, c, :, n * 128 : (n + 1) * 128] = block.astype(jnp.bfloat16)
        return carry

    lax.fori_loop(0, cols, column, 0, unroll=4)


def spread_kernel(dims, pack, bundle, winds, obs, zs, zr, xs, xr, hs, hr, gs, gr, os, orr, local):
    sections, bands, cols, halo = dims
    me = lax.axis_index("tm")
    band = lax.axis_index("lon")
    core = lax.axis_index("probe")
    half = cols // 2
    sides = (band, lax.rem(band + 1, bands), lax.rem(band + bands - 1, bands))

    def remote(src, dst, send, recv, tm, lon, probe):
        copy = pltpu.make_async_remote_copy(
            src_ref=src, dst_ref=dst, send_sem=send, recv_sem=recv,
            device_id={"tm": tm, "lon": lon, "probe": probe},
            device_id_type=pl.DeviceIdType.MESH,
        )
        copy.start()
        return copy

    barrier = pltpu.get_barrier_semaphore()
    for k in range(sections):
        tm = lax.rem(me + k, sections)
        for n, lon in enumerate(sides):
            if k or n:
                pl.semaphore_signal(
                    barrier, inc=1, device_id={"tm": tm, "lon": lon, "probe": core},
                    device_id_type=pl.DeviceIdType.MESH,
                )
    pl.semaphore_signal(
        barrier, inc=1, device_id={"tm": me, "lon": band, "probe": 1 - core},
        device_id_type=pl.DeviceIdType.MESH,
    )
    own_winds = pltpu.make_async_copy(pack.at[me], winds.at[me, :, pl.ds(halo, cols)], local.at[0])
    own_winds.start()
    own_obs = pltpu.make_async_copy(bundle, obs.at[me, 0], local.at[1])
    own_obs.start()
    pl.semaphore_wait(barrier, 3 * sections)

    mine = pl.ds(halo + half * core, half)
    beside = lax.rem(band + bands + 2 * core - 1, bands)
    copies = []
    for k in range(1, sections):
        tm = lax.rem(me + k, sections)
        copies.append(
            remote(
                pack.at[tm, :, pl.ds(half * core, half)], winds.at[me, :, mine],
                zs.at[k], zr.at[me], tm, band, core,
            )
        )
    for k in range(sections):
        tm = lax.rem(me + k, sections)
        for n, lon in enumerate(sides):
            if k or n:
                copies.append(
                    remote(
                        bundle, obs.at[me, n], os.at[3 * k + n], orr.at[3 * me + n], tm, lon, core
                    )
                )
    own_winds.wait()
    own_obs.wait()

    def described(src, dst, send, recv, lon, probe):
        return pltpu.make_async_remote_copy(
            src_ref=src, dst_ref=dst, send_sem=send, recv_sem=recv,
            device_id={"tm": me, "lon": lon, "probe": probe},
            device_id_type=pl.DeviceIdType.MESH,
        )

    def z_copy(s):
        place = winds.at[s, :, mine]
        return described(place, place, zs.at[0], zr.at[s], beside, core)

    def h_copy(s):
        place = winds.at[s, :, mine]
        return described(place, place, hs.at[s], hr.at[s], band, 1 - core)

    def x_copy(s, depth):
        src = winds.at[s, :, pl.ds(halo + core * (cols - depth), depth)]
        dst = winds.at[s, :, pl.ds(halo - depth + (1 - core) * (cols + depth), depth)]
        return (
            described(src, dst, xs.at[s], xr.at[s], beside, core),
            described(dst, dst, gs.at[s], gr.at[s], band, 1 - core),
        )

    depths = [min(halo, (s + 1) * winds.shape[1]) for s in range(sections)]
    edges = [x_copy(s, depths[s]) for s in range(sections)]
    order = range(sections - 1, -1, -1)
    for s in order:

        @pl.when(me == s)
        def _():
            edges[s][0].start()

    for s in order:

        @pl.when(me != s)
        def _():
            z_copy(s).wait_recv()
            copy = h_copy(s)
            copy.start()
            if depths[s] > half:
                copy.wait_recv()
            edges[s][0].start()

    for s in order:
        edges[s][0].wait_recv()
        edges[s][1].start()
    for s in order:

        @pl.when(me != s)
        def _():
            copy = h_copy(s)
            if depths[s] <= half:
                copy.wait_recv()
            copy.wait_send()

        edges[s][0].wait_send()
        edges[s][1].wait()
    for copy in copies:
        copy.wait_send()
    for k in range(sections):
        source = lax.rem(me + k, sections)
        for n in range(3):
            if k or n:
                place = obs.at[source, n]
                described(
                    place, place, os.at[0], orr.at[3 * source + n], beside, core
                ).wait_recv()


def on_device(winds, mixing, obs_cell, obs_weight, probe_sign, week_map, prior_precision):
    hours_sec = winds.shape[2]
    levels = winds.shape[3]
    band_cols = winds.shape[4]
    lat_rows = winds.shape[5]
    probes = probe_sign.shape[0]
    week_count, _, own = prior_precision.shape
    sections = lax.axis_size("tm")
    bands = lax.axis_size("lon")
    hours = sections * hours_sec
    lev_pad = -(-levels // 8) * 8
    halo = -(-hours // 4) * 4
    left = hours
    window = -(-(own + 2 * hours) // 64) * 64
    lanes = window * probes

    shape = (hours_sec, sections, band_cols, lev_pad, 2 * window)
    pack = pl.pallas_call(
        functools.partial(
            window_kernel, (levels, lev_pad, band_cols, lat_rows, own, left, window)
        ),
        out_shape=jax.ShapeDtypeStruct((sections, hours_sec) + shape[2:], jnp.bfloat16),
        grid=(hours_sec, sections),
        in_specs=[
            pl.BlockSpec(
                (2, 1, 1, levels, band_cols, lat_rows), lambda h, d: (0, 0, h, 0, 0, 0)
            )
        ],
        out_specs=pl.BlockSpec((1, 1) + shape[2:], lambda h, d: (d, h, 0, 0, 0)),
        scratch_shapes=[pltpu.VMEM((band_cols * lev_pad, 128), jnp.float32)]
        * (2 * window // 128),
        compiler_params=pltpu.CompilerParams(vmem_limit_bytes=40 << 20),
    )(winds)

    value = (2 * probe_sign[:, 0, 0] - 1).astype(jnp.float32) * obs_weight[0, 0][None]
    count = value.shape[1]
    week_row = jnp.pad(week_map.astype(jnp.float32), ((0, 0), (0, count - hours_sec)))
    bundle = jnp.concatenate([obs_cell[0].astype(jnp.float32), value, week_row], axis=0)
    ext_cols = band_cols + 2 * halo
    sem = pltpu.SemaphoreType.DMA
    w, obs = pl.pallas_call(
        functools.partial(spread_kernel, (sections, bands, band_cols, halo)),
        out_shape=(
            jax.ShapeDtypeStruct(
                (sections, hours_sec, ext_cols, lev_pad, 2 * window), jnp.bfloat16
            ),
            jax.ShapeDtypeStruct((sections, 3) + bundle.shape, jnp.float32),
        ),
        in_specs=[pl.BlockSpec(memory_space=pl.ANY)] * 2,
        out_specs=(pl.BlockSpec(memory_space=pl.ANY),) * 2,
        scratch_shapes=[sem((sections,))] * 8 + [sem((3 * sections,))] * 2 + [sem((2,))],
        compiler_params=pltpu.CompilerParams(collective_id=0, has_side_effects=True),
    )(pack, bundle)
    w = w.reshape((hours,) + w.shape[2:])
    weeks = obs[:, 0, 1 + probes, :hours_sec].astype(jnp.int32).reshape(hours)

    mix = jnp.pad(mixing.T, ((0, lev_pad - levels),) * 2)
    high_mix = lax.reduce_precision(mix, 8, 7)
    mix = jnp.concatenate([high_mix, mix - high_mix, high_mix], axis=1).astype(jnp.bfloat16)

    dims = (
        hours, hours_sec, halo, band_cols, levels, lev_pad, lat_rows, own, left, window, probes
    )
    estimate = pl.pallas_call(
        functools.partial(sweep_kernel, dims),
        out_shape=jax.ShapeDtypeStruct((week_count, band_cols, lanes), jnp.float32),
        grid_spec=pltpu.PrefetchScalarGridSpec(
            num_scalar_prefetch=1,
            grid=(hours,),
            in_specs=[
                pl.BlockSpec(mix.shape, lambda i, wk: (0, 0)),
                pl.BlockSpec((1,) + w.shape[1:], lambda i, wk: (hours - 1 - i, 0, 0, 0)),
                pl.BlockSpec(
                    (1,) + obs.shape[1:], lambda i, wk: ((hours - 1 - i) // hours_sec, 0, 0, 0)
                ),
            ],
            out_specs=pl.BlockSpec((week_count, band_cols, lanes), lambda i, wk: (0, 0, 0)),
            scratch_shapes=[
                pltpu.VMEM((ext_cols, lev_pad, lanes), jnp.float32),
                pltpu.VMEM((ext_cols, lev_pad, lanes), jnp.float32),
                pltpu.VMEM((week_count, band_cols, lanes), jnp.float32),
            ],
        ),
        compiler_params=pltpu.CompilerParams(vmem_limit_bytes=48 << 20),
    )(weeks, mix, w, obs)
    return (prior_precision + estimate[..., left : left + own])[None]


def solution(mesh):
    placed = (
        P(None, ("groups", "tm"), None, None, "lon", None),
        P(),
        P(("groups", "tm"), "lon", None),
        P(("groups", "tm"), "lon", None),
        P("probe", ("groups", "tm"), "lon", None),
        P(("groups", "tm"), None),
        P("groups", "lon", "tm"),
    )
    return jax.shard_map(
        on_device,
        mesh=mesh,
        in_specs=placed,
        out_specs=P("probe", "groups", "lon", "tm"),
        check_vma=False,
    )
```

```python
import functools

import jax
import jax.numpy as jnp
from jax import lax
from jax.experimental import pallas as pl
from jax.experimental.pallas import tpu as pltpu
from jax.sharding import PartitionSpec as P


def split2(x):
    high = x.astype(jnp.bfloat16)
    low = (x - high.astype(jnp.float32)).astype(jnp.bfloat16)
    return high, low


def sweep_kernel(dims, weeks_ref, mix_ref, winds_ref, obs_ref, out_ref, state, mixed, flux):
    hours, hours_sec, halo, band_cols, lev, lev_pad, lat_rows, own, left, window, probes = dims
    ext_cols = band_cols + 2 * halo
    lanes = window * probes
    step = pl.program_id(0)
    hour = hours - 1 - step
    first_row = lax.axis_index("tm") * own - left

    @pl.when(step == 0)
    def _():
        state[...] = jnp.zeros_like(state)
        mixed[...] = jnp.zeros_like(mixed)
        flux[...] = jnp.zeros_like(flux)

    @pl.when(lax.rem(hour, hours_sec) == 0)
    def _():
        count = obs_ref.shape[-1]
        for piece, (begin, width, shift) in enumerate(
            ((halo, band_cols, 0), (0, halo, -band_cols), (halo + band_cols, halo, band_cols))
        ):
            cell = obs_ref[0, piece, 0:1, :].astype(jnp.int32)
            level = cell // (band_cols * lat_rows)
            rest = cell - level * (band_cols * lat_rows)
            column = rest // lat_rows
            row = rest - column * lat_rows - first_row
            place = (column + halo + shift - begin) * lev_pad + level
            sub = lax.broadcasted_iota(jnp.int32, (window, count), 0)
            hit = sub == row
            parts = [
                split2(jnp.where(hit, obs_ref[0, piece, 1 + p : 2 + p, :], 0.0))
                for p in range(probes)
            ]
            rhs = jnp.concatenate([x[0] for x in parts] + [x[1] for x in parts], axis=0)
            cols_at = max(n for n in range(1, 19) if width % n == 0)
            chunk = lax.broadcasted_iota(jnp.int32, (cols_at * lev_pad, count), 0)

            def body(i, carry):
                hot = (chunk == place - i * (cols_at * lev_pad)).astype(jnp.float32)
                got = lax.dot_general(
                    hot.astype(jnp.bfloat16), rhs, (((1,), (1,)), ((), ())),
                    preferred_element_type=jnp.float32,
                )
                add = got[:, :lanes] + got[:, lanes:]
                for c in range(cols_at):
                    at = begin + i * cols_at + c
                    state[at] += add[c * lev_pad : (c + 1) * lev_pad]
                return carry

            trips = width // cols_at
            if piece:
                trips = jnp.where(hour > 0, trips, 0)
            lax.fori_loop(0, trips, body, 0)

    week = weeks_ref[hour]
    flux[week] += state[halo : halo + band_cols, 0, :]

    @pl.when(hour > 0)
    def _():
        mix = mix_ref[...]
        wide = 8
        deep = 4

        def mixing(i, carry):
            at = jnp.minimum(halo - hour + i * wide, ext_cols - wide)
            for c in range(0, wide, 2):
                x = jnp.concatenate([state[at + c], state[at + c + 1]], axis=1)
                low = x - x.astype(jnp.bfloat16).astype(jnp.float32)
                stack = jnp.concatenate([x, x, low], axis=0).astype(jnp.bfloat16)
                got = jnp.dot(mix, stack, preferred_element_type=jnp.float32)
                mixed[at + c] = got[:, :lanes]
                mixed[at + c + 1] = got[:, lanes:]
            return carry

        lax.fori_loop(0, (band_cols + 2 * hour + wide - 1) // wide, mixing, 0)

        lane = lax.broadcasted_iota(jnp.int32, (lev_pad, lanes), 1)
        first = lane < window
        grid_row = lax.rem(lane, window) + first_row
        keep = jnp.logical_and(grid_row >= 0, grid_row < lat_rows - 1)

        def advect(i, carry):
            at = jnp.minimum(halo - hour + 1 + i * deep, ext_cols - 1 - deep)
            packed = winds_ref[0, at - 1].astype(jnp.float32)
            west = jnp.where(first, packed, pltpu.roll(packed, window, 1))
            before, here = mixed[at - 1], mixed[at]
            for c in range(deep):
                after = mixed[at + c + 1]
                packed = winds_ref[0, at + c].astype(jnp.float32)
                turned = pltpu.roll(packed, window, 1)
                east = jnp.where(first, packed, turned)
                north = jnp.where(keep, jnp.where(first, turned, packed), 0.0)
                south = pltpu.roll(north, 1, 1)
                g = (
                    here
                    + jnp.maximum(east, 0.0) * (after - here)
                    + jnp.minimum(west, 0.0) * (here - before)
                )
                above = pltpu.roll(g, lanes - 1, 1)
                below = pltpu.roll(g, 1, 1)
                state[at + c] = (
                    g + jnp.maximum(north, 0.0) * (above - g) + jnp.minimum(south, 0.0) * (g - below)
                )
                before, here, west = here, after, east
            return carry

        lax.fori_loop(0, (band_cols + 2 * hour - 2 + deep - 1) // deep, advect, 0)

    @pl.when(step == hours - 1)
    def _():
        square = flux[...] * flux[...]
        rolled = [
            square[w] + pltpu.roll(square[w], lanes - window, 1) for w in range(square.shape[0])
        ]
        for w in range(square.shape[0]):
            out_ref[w] = rolled[w] * 0.5


def window_kernel(dims, winds_ref, out_ref, *tmp):
    sections, lev, lev_pad, cols, lat, own, left, window = dims
    lane = lax.broadcasted_iota(jnp.int32, (cols, 128), 1)

    @pl.when((pl.program_id(0) == 0) & (pl.program_id(1) == 0))
    def _():
        for part in tmp:
            part[...] = jnp.zeros_like(part)

    def tile(comp, i, v):
        x = winds_ref[comp, 0, 0, i, :, v * 128 : min(v * 128 + 128, lat)].astype(jnp.float32)
        if x.shape[1] < 128:
            x = jnp.concatenate([x, jnp.zeros((cols, 128 - x.shape[1]), jnp.float32)], axis=1)
        return x

    def fill(start):
        def level(i, carry):
            for n, part in enumerate(tmp):
                both = jnp.zeros((cols, 128), jnp.float32)
                for comp in range(2):
                    base = comp * window - start
                    for v in range(-(-lat // 128)):
                        low = max(comp * window, base + v * 128, n * 128)
                        high = min((comp + 1) * window, base + min(v * 128 + 128, lat), n * 128 + 128)
                        if low < high:
                            x = tile(comp, i, v)
                            if base % 128:
                                x = pltpu.roll(x, base % 128, 1)
                            inside = (lane >= low - n * 128) & (lane < high - n * 128)
                            both = jnp.where(inside, x, both)
                part[pl.ds(i, cols, stride=lev_pad), :] = both
            return carry

        lax.fori_loop(0, lev, level, 0, unroll=4)

    for d in range(sections):
        pl.when(pl.program_id(1) == d)(functools.partial(fill, d * own - left))

    def column(c, carry):
        for n, part in enumerate(tmp):
            block = part[pl.ds(pl.multiple_of(c * lev_pad, 8), lev_pad), :]
            out_ref[0, 0, c, :, n * 128 : (n + 1) * 128] = block.astype(jnp.bfloat16)
        return carry

    lax.fori_loop(0, cols, column, 0, unroll=4)


def spread_kernel(dims, pack, bundle, winds, obs, zs, zr, xs, xr, hs, hr, gs, gr, os, orr, local):
    sections, bands, cols, halo = dims
    me = lax.axis_index("tm")
    band = lax.axis_index("lon")
    core = lax.axis_index("probe")
    half = cols // 2
    sides = (band, lax.rem(band + 1, bands), lax.rem(band + bands - 1, bands))

    def remote(src, dst, send, recv, tm, lon, probe):
        copy = pltpu.make_async_remote_copy(
            src_ref=src, dst_ref=dst, send_sem=send, recv_sem=recv,
            device_id={"tm": tm, "lon": lon, "probe": probe},
            device_id_type=pl.DeviceIdType.MESH,
        )
        copy.start()
        return copy

    barrier = pltpu.get_barrier_semaphore()
    for k in range(sections):
        tm = lax.rem(me + k, sections)
        for n, lon in enumerate(sides):
            if k or n:
                pl.semaphore_signal(
                    barrier, inc=1, device_id={"tm": tm, "lon": lon, "probe": core},
                    device_id_type=pl.DeviceIdType.MESH,
                )
    pl.semaphore_signal(
        barrier, inc=1, device_id={"tm": me, "lon": band, "probe": 1 - core},
        device_id_type=pl.DeviceIdType.MESH,
    )
    own_winds = pltpu.make_async_copy(pack.at[me], winds.at[me, :, pl.ds(halo, cols)], local.at[0])
    own_winds.start()
    own_obs = pltpu.make_async_copy(bundle, obs.at[me, 0], local.at[1])
    own_obs.start()
    pl.semaphore_wait(barrier, 3 * sections)

    mine = pl.ds(halo + half * core, half)
    beside = lax.rem(band + bands + 2 * core - 1, bands)
    copies = []
    hours_sec = winds.shape[1]
    hours = range(hours_sec - 1, -1, -1)
    for h in hours:
        for k in range(1, sections):
            tm = lax.rem(me + k, sections)
            copies.append(
                remote(
                    pack.at[tm, h, pl.ds(half * core, half)], winds.at[me, h, mine],
                    zs.at[k * hours_sec + h], zr.at[me * hours_sec + h], tm, band, core,
                )
            )
    for k in range(sections):
        tm = lax.rem(me + k, sections)
        for n, lon in enumerate(sides):
            if k or n:
                copies.append(
                    remote(
                        bundle, obs.at[me, n], os.at[3 * k + n], orr.at[3 * me + n], tm, lon, core
                    )
                )
    own_winds.wait()
    own_obs.wait()

    def described(src, dst, send, recv, lon, probe):
        return pltpu.make_async_remote_copy(
            src_ref=src, dst_ref=dst, send_sem=send, recv_sem=recv,
            device_id={"tm": me, "lon": lon, "probe": probe},
            device_id_type=pl.DeviceIdType.MESH,
        )

    def z_copy(s, h):
        place = winds.at[s, h, mine]
        return described(place, place, zs.at[0], zr.at[s * hours_sec + h], beside, core)

    def h_copy(s, h):
        place = winds.at[s, h, mine]
        at = s * hours_sec + h
        return described(place, place, hs.at[at], hr.at[at], band, 1 - core)

    depths = [min(halo, (s + 1) * hours_sec) for s in range(sections)]

    def x_copy(s, h):
        depth = depths[s]
        at = s * hours_sec + h
        src = winds.at[s, h, pl.ds(halo + core * (cols - depth), depth)]
        dst = winds.at[s, h, pl.ds(halo - depth + (1 - core) * (cols + depth), depth)]
        return (
            described(src, dst, xs.at[at], xr.at[at], beside, core),
            described(dst, dst, gs.at[at], gr.at[at], band, 1 - core),
        )

    order = [(s, h) for h in hours for s in range(sections - 1, -1, -1)]
    edges = {at: x_copy(*at) for at in order}
    for at in order:

        @pl.when(me == at[0])
        def _():
            edges[at][0].start()

    for at in order:

        @pl.when(me != at[0])
        def _():
            z_copy(*at).wait_recv()
            copy = h_copy(*at)
            copy.start()
            if depths[at[0]] > half:
                copy.wait_recv()
            edges[at][0].start()

    for at in order:
        edges[at][0].wait_recv()
        edges[at][1].start()
    for at in order:

        @pl.when(me != at[0])
        def _():
            copy = h_copy(*at)
            if depths[at[0]] <= half:
                copy.wait_recv()
            copy.wait_send()

        edges[at][0].wait_send()
        edges[at][1].wait()
    for copy in copies:
        copy.wait_send()
    for k in range(sections):
        source = lax.rem(me + k, sections)
        for n in range(3):
            if k or n:
                place = obs.at[source, n]
                described(
                    place, place, os.at[0], orr.at[3 * source + n], beside, core
                ).wait_recv()


def on_device(winds, mixing, obs_cell, obs_weight, probe_sign, week_map, prior_precision):
    hours_sec = winds.shape[2]
    levels = winds.shape[3]
    band_cols = winds.shape[4]
    lat_rows = winds.shape[5]
    probes = probe_sign.shape[0]
    week_count, _, own = prior_precision.shape
    sections = lax.axis_size("tm")
    bands = lax.axis_size("lon")
    hours = sections * hours_sec
    lev_pad = -(-levels // 8) * 8
    halo = -(-hours // 4) * 4
    left = hours
    window = -(-(own + 2 * hours) // 64) * 64
    lanes = window * probes

    shape = (hours_sec, sections, band_cols, lev_pad, 2 * window)
    pack = pl.pallas_call(
        functools.partial(
            window_kernel, (sections, levels, lev_pad, band_cols, lat_rows, own, left, window)
        ),
        out_shape=jax.ShapeDtypeStruct((sections, hours_sec) + shape[2:], jnp.bfloat16),
        grid=(hours_sec, sections),
        in_specs=[
            pl.BlockSpec(
                (2, 1, 1, levels, band_cols, lat_rows), lambda h, d: (0, 0, h, 0, 0, 0)
            )
        ],
        out_specs=pl.BlockSpec((1, 1) + shape[2:], lambda h, d: (d, h, 0, 0, 0)),
        scratch_shapes=[pltpu.VMEM((band_cols * lev_pad, 128), jnp.float32)]
        * (2 * window // 128),
        compiler_params=pltpu.CompilerParams(vmem_limit_bytes=40 << 20),
    )(winds)

    value = (2 * probe_sign[:, 0, 0] - 1).astype(jnp.float32) * obs_weight[0, 0][None]
    count = value.shape[1]
    week_row = jnp.pad(week_map.astype(jnp.float32), ((0, 0), (0, count - hours_sec)))
    bundle = jnp.concatenate([obs_cell[0].astype(jnp.float32), value, week_row], axis=0)
    ext_cols = band_cols + 2 * halo
    sem = pltpu.SemaphoreType.DMA
    w, obs = pl.pallas_call(
        functools.partial(spread_kernel, (sections, bands, band_cols, halo)),
        out_shape=(
            jax.ShapeDtypeStruct(
                (sections, hours_sec, ext_cols, lev_pad, 2 * window), jnp.bfloat16
            ),
            jax.ShapeDtypeStruct((sections, 3) + bundle.shape, jnp.float32),
        ),
        in_specs=[pl.BlockSpec(memory_space=pl.ANY)] * 2,
        out_specs=(pl.BlockSpec(memory_space=pl.ANY),) * 2,
        scratch_shapes=[sem((hours,))] * 8 + [sem((3 * sections,))] * 2 + [sem((2,))],
        compiler_params=pltpu.CompilerParams(collective_id=0, has_side_effects=True),
    )(pack, bundle)
    w = w.reshape((hours,) + w.shape[2:])
    weeks = obs[:, 0, 1 + probes, :hours_sec].astype(jnp.int32).reshape(hours)

    mix = jnp.pad(mixing.T, ((0, lev_pad - levels),) * 2)
    high_mix = lax.reduce_precision(mix, 8, 7)
    mix = jnp.concatenate([high_mix, mix - high_mix, high_mix], axis=1).astype(jnp.bfloat16)

    dims = (
        hours, hours_sec, halo, band_cols, levels, lev_pad, lat_rows, own, left, window, probes
    )
    estimate = pl.pallas_call(
        functools.partial(sweep_kernel, dims),
        out_shape=jax.ShapeDtypeStruct((week_count, band_cols, lanes), jnp.float32),
        grid_spec=pltpu.PrefetchScalarGridSpec(
            num_scalar_prefetch=1,
            grid=(hours,),
            in_specs=[
                pl.BlockSpec(mix.shape, lambda i, wk: (0, 0)),
                pl.BlockSpec((1,) + w.shape[1:], lambda i, wk: (hours - 1 - i, 0, 0, 0)),
                pl.BlockSpec(
                    (1,) + obs.shape[1:], lambda i, wk: ((hours - 1 - i) // hours_sec, 0, 0, 0)
                ),
            ],
            out_specs=pl.BlockSpec((week_count, band_cols, lanes), lambda i, wk: (0, 0, 0)),
            scratch_shapes=[
                pltpu.VMEM((ext_cols, lev_pad, lanes), jnp.float32),
                pltpu.VMEM((ext_cols, lev_pad, lanes), jnp.float32),
                pltpu.VMEM((week_count, band_cols, lanes), jnp.float32),
            ],
        ),
        compiler_params=pltpu.CompilerParams(vmem_limit_bytes=48 << 20),
    )(weeks, mix, w, obs)
    return (prior_precision + estimate[..., left : left + own])[None]


def solution(mesh):
    placed = (
        P(None, ("groups", "tm"), None, None, "lon", None),
        P(),
        P(("groups", "tm"), "lon", None),
        P(("groups", "tm"), "lon", None),
        P("probe", ("groups", "tm"), "lon", None),
        P(("groups", "tm"), None),
        P("groups", "lon", "tm"),
    )
    return jax.shard_map(
        on_device,
        mesh=mesh,
        in_specs=placed,
        out_specs=P("probe", "groups", "lon", "tm"),
        check_vma=False,
    )
```

```python
import functools

import jax
import jax.numpy as jnp
from jax import lax
from jax.experimental import pallas as pl
from jax.experimental.pallas import tpu as pltpu
from jax.sharding import PartitionSpec as P


def split2(x):
    high = x.astype(jnp.bfloat16)
    low = (x - high.astype(jnp.float32)).astype(jnp.bfloat16)
    return high, low


def sweep_kernel(dims, weeks_ref, mix_ref, winds_ref, obs_ref, out_ref, state, mixed, flux):
    hours, hours_sec, halo, band_cols, lev, lev_pad, lat_rows, own, left, window, probes = dims
    ext_cols = band_cols + 2 * halo
    lanes = window * probes
    step = pl.program_id(0)
    hour = hours - 1 - step
    first_row = lax.axis_index("tm") * own - left

    @pl.when(step == 0)
    def _():
        state[...] = jnp.zeros_like(state)
        mixed[...] = jnp.zeros_like(mixed)
        flux[...] = jnp.zeros_like(flux)

    count = obs_ref.shape[-1]

    def observed(piece):
        cell = obs_ref[0, piece, 0:1, :].astype(jnp.int32)
        level = cell // (band_cols * lat_rows)
        rest = cell - level * (band_cols * lat_rows)
        column = rest // lat_rows
        row = rest - column * lat_rows - first_row
        hit = lax.broadcasted_iota(jnp.int32, (window, count), 0) == row
        parts = [
            split2(jnp.where(hit, obs_ref[0, piece, 1 + p : 2 + p, :], 0.0)) for p in range(probes)
        ]
        rhs = jnp.concatenate([x[0] for x in parts] + [x[1] for x in parts], axis=0)
        return level, column, rhs

    def placed_sum(hot, rhs):
        got = lax.dot_general(
            hot.astype(jnp.float32).astype(jnp.bfloat16), rhs, (((1,), (1,)), ((), ())),
            preferred_element_type=jnp.float32,
        )
        return got[:, :lanes] + got[:, lanes:]

    week = weeks_ref[hour]

    @pl.when((lax.rem(hour, hours_sec) == 0) & (hour > 0))
    def _():
        for piece, (begin, width, shift) in enumerate(
            ((halo, band_cols, 0), (0, halo, -band_cols), (halo + band_cols, halo, band_cols))
        ):
            level, column, rhs = observed(piece)
            place = (column + halo + shift - begin) * lev_pad + level
            cols_at = max(n for n in range(1, 19) if width % n == 0)
            chunk = lax.broadcasted_iota(jnp.int32, (cols_at * lev_pad, count), 0)

            def body(i, carry):
                add = placed_sum(chunk == place - i * (cols_at * lev_pad), rhs)
                for c in range(cols_at):
                    at = begin + i * cols_at + c
                    state[at] += add[c * lev_pad : (c + 1) * lev_pad]
                return carry

            lax.fori_loop(0, width // cols_at, body, 0)

    @pl.when(hour == 0)
    def _():
        level, column, rhs = observed(0)
        high = -(-band_cols // 8) * 8
        chunk = lax.broadcasted_iota(jnp.int32, (high, count), 0)
        add = placed_sum(chunk == jnp.where(level == 0, column, -1), rhs)
        flux[week] += add[:band_cols]

    flux[week] += state[halo : halo + band_cols, 0, :]

    @pl.when(hour > 0)
    def _():
        mix = mix_ref[...]
        wide = 8
        deep = 4

        def mixing(i, carry):
            at = jnp.minimum(halo - hour + i * wide, ext_cols - wide)
            for c in range(0, wide, 2):
                x = jnp.concatenate([state[at + c], state[at + c + 1]], axis=1)
                low = x - x.astype(jnp.bfloat16).astype(jnp.float32)
                stack = jnp.concatenate([x, x, low], axis=0).astype(jnp.bfloat16)
                got = jnp.dot(mix, stack, preferred_element_type=jnp.float32)
                mixed[at + c] = got[:, :lanes]
                mixed[at + c + 1] = got[:, lanes:]
            return carry

        lax.fori_loop(0, (band_cols + 2 * hour + wide - 1) // wide, mixing, 0)

        lane = lax.broadcasted_iota(jnp.int32, (lev_pad, lanes), 1)
        first = lane < window
        grid_row = lax.rem(lane, window) + first_row
        keep = jnp.logical_and(grid_row >= 0, grid_row < lat_rows - 1)

        def advect(i, carry):
            at = jnp.minimum(halo - hour + 1 + i * deep, ext_cols - 1 - deep)
            packed = winds_ref[0, at - 1].astype(jnp.float32)
            west = jnp.where(first, packed, pltpu.roll(packed, window, 1))
            before, here = mixed[at - 1], mixed[at]
            for c in range(deep):
                after = mixed[at + c + 1]
                packed = winds_ref[0, at + c].astype(jnp.float32)
                turned = pltpu.roll(packed, window, 1)
                east = jnp.where(first, packed, turned)
                north = jnp.where(keep, jnp.where(first, turned, packed), 0.0)
                south = pltpu.roll(north, 1, 1)
                g = (
                    here
                    + jnp.maximum(east, 0.0) * (after - here)
                    + jnp.minimum(west, 0.0) * (here - before)
                )
                above = pltpu.roll(g, lanes - 1, 1)
                below = pltpu.roll(g, 1, 1)
                state[at + c] = (
                    g + jnp.maximum(north, 0.0) * (above - g) + jnp.minimum(south, 0.0) * (g - below)
                )
                before, here, west = here, after, east
            return carry

        lax.fori_loop(0, (band_cols + 2 * hour - 2 + deep - 1) // deep, advect, 0)

    @pl.when(step == hours - 1)
    def _():
        square = flux[...] * flux[...]
        rolled = [
            square[w] + pltpu.roll(square[w], lanes - window, 1) for w in range(square.shape[0])
        ]
        for w in range(square.shape[0]):
            out_ref[w] = rolled[w] * 0.5


def window_kernel(dims, winds_ref, out_ref, *tmp):
    sections, lev, lev_pad, cols, lat, own, left, window = dims
    lane = lax.broadcasted_iota(jnp.int32, (cols, 128), 1)

    @pl.when((pl.program_id(0) == 0) & (pl.program_id(1) == 0))
    def _():
        for part in tmp:
            part[...] = jnp.zeros_like(part)

    def tile(comp, i, v):
        x = winds_ref[comp, 0, 0, i, :, v * 128 : min(v * 128 + 128, lat)].astype(jnp.float32)
        if x.shape[1] < 128:
            x = jnp.concatenate([x, jnp.zeros((cols, 128 - x.shape[1]), jnp.float32)], axis=1)
        return x

    def fill(start):
        def level(i, carry):
            for n, part in enumerate(tmp):
                both = jnp.zeros((cols, 128), jnp.float32)
                for comp in range(2):
                    base = comp * window - start
                    for v in range(-(-lat // 128)):
                        low = max(comp * window, base + v * 128, n * 128)
                        high = min((comp + 1) * window, base + min(v * 128 + 128, lat), n * 128 + 128)
                        if low < high:
                            x = tile(comp, i, v)
                            if base % 128:
                                x = pltpu.roll(x, base % 128, 1)
                            inside = (lane >= low - n * 128) & (lane < high - n * 128)
                            both = jnp.where(inside, x, both)
                part[pl.ds(i, cols, stride=lev_pad), :] = both
            return carry

        lax.fori_loop(0, lev, level, 0, unroll=4)

    for d in range(sections):
        pl.when(pl.program_id(1) == d)(functools.partial(fill, d * own - left))

    def column(c, carry):
        for n, part in enumerate(tmp):
            block = part[pl.ds(pl.multiple_of(c * lev_pad, 8), lev_pad), :]
            out_ref[0, 0, c, :, n * 128 : (n + 1) * 128] = block.astype(jnp.bfloat16)
        return carry

    lax.fori_loop(0, cols, column, 0, unroll=4)


def spread_kernel(dims, pack, bundle, winds, obs, zs, zr, xs, xr, hs, hr, gs, gr, os, orr, local):
    sections, bands, cols, halo = dims
    me = lax.axis_index("tm")
    band = lax.axis_index("lon")
    core = lax.axis_index("probe")
    half = cols // 2
    sides = (band, lax.rem(band + 1, bands), lax.rem(band + bands - 1, bands))

    def remote(src, dst, send, recv, tm, lon, probe):
        copy = pltpu.make_async_remote_copy(
            src_ref=src, dst_ref=dst, send_sem=send, recv_sem=recv,
            device_id={"tm": tm, "lon": lon, "probe": probe},
            device_id_type=pl.DeviceIdType.MESH,
        )
        copy.start()
        return copy

    barrier = pltpu.get_barrier_semaphore()
    for k in range(sections):
        tm = lax.rem(me + k, sections)
        for n, lon in enumerate(sides):
            if k or n:
                pl.semaphore_signal(
                    barrier, inc=1, device_id={"tm": tm, "lon": lon, "probe": core},
                    device_id_type=pl.DeviceIdType.MESH,
                )
    pl.semaphore_signal(
        barrier, inc=1, device_id={"tm": me, "lon": band, "probe": 1 - core},
        device_id_type=pl.DeviceIdType.MESH,
    )
    own_winds = pltpu.make_async_copy(pack.at[me], winds.at[me, :, pl.ds(halo, cols)], local.at[0])
    own_winds.start()
    own_obs = pltpu.make_async_copy(bundle, obs.at[me, 0], local.at[1])
    own_obs.start()
    pl.semaphore_wait(barrier, 3 * sections)

    mine = pl.ds(halo + half * core, half)
    beside = lax.rem(band + bands + 2 * core - 1, bands)
    copies = []
    hours_sec = winds.shape[1]
    hours = range(hours_sec - 1, -1, -1)
    for h in hours:
        for k in range(1, sections):
            tm = lax.rem(me + k, sections)
            copies.append(
                remote(
                    pack.at[tm, h, pl.ds(half * core, half)], winds.at[me, h, mine],
                    zs.at[k * hours_sec + h], zr.at[me * hours_sec + h], tm, band, core,
                )
            )
    for k in range(sections):
        tm = lax.rem(me + k, sections)
        for n, lon in enumerate(sides):
            if k or n:
                copies.append(
                    remote(
                        bundle, obs.at[me, n], os.at[3 * k + n], orr.at[3 * me + n], tm, lon, core
                    )
                )
    own_winds.wait()
    own_obs.wait()

    def described(src, dst, send, recv, lon, probe):
        return pltpu.make_async_remote_copy(
            src_ref=src, dst_ref=dst, send_sem=send, recv_sem=recv,
            device_id={"tm": me, "lon": lon, "probe": probe},
            device_id_type=pl.DeviceIdType.MESH,
        )

    def z_copy(s, h):
        place = winds.at[s, h, mine]
        return described(place, place, zs.at[0], zr.at[s * hours_sec + h], beside, core)

    def h_copy(s, h):
        place = winds.at[s, h, mine]
        at = s * hours_sec + h
        return described(place, place, hs.at[at], hr.at[at], band, 1 - core)

    depths = [min(halo, (s + 1) * hours_sec) for s in range(sections)]

    def x_copy(s, h):
        depth = depths[s]
        at = s * hours_sec + h
        src = winds.at[s, h, pl.ds(halo + core * (cols - depth), depth)]
        dst = winds.at[s, h, pl.ds(halo - depth + (1 - core) * (cols + depth), depth)]
        return (
            described(src, dst, xs.at[at], xr.at[at], beside, core),
            described(dst, dst, gs.at[at], gr.at[at], band, 1 - core),
        )

    order = [(s, h) for h in hours for s in range(sections - 1, -1, -1)]
    edges = {at: x_copy(*at) for at in order}
    for at in order:

        @pl.when(me == at[0])
        def _():
            edges[at][0].start()

    for at in order:

        @pl.when(me != at[0])
        def _():
            z_copy(*at).wait_recv()
            copy = h_copy(*at)
            copy.start()
            if depths[at[0]] > half:
                copy.wait_recv()
            edges[at][0].start()

    for at in order:
        edges[at][0].wait_recv()
        edges[at][1].start()
    for at in order:

        @pl.when(me != at[0])
        def _():
            copy = h_copy(*at)
            if depths[at[0]] <= half:
                copy.wait_recv()
            copy.wait_send()

        edges[at][0].wait_send()
        edges[at][1].wait()
    for copy in copies:
        copy.wait_send()
    for k in range(sections):
        source = lax.rem(me + k, sections)
        for n in range(3):
            if k or n:
                place = obs.at[source, n]
                described(
                    place, place, os.at[0], orr.at[3 * source + n], beside, core
                ).wait_recv()


def on_device(winds, mixing, obs_cell, obs_weight, probe_sign, week_map, prior_precision):
    hours_sec = winds.shape[2]
    levels = winds.shape[3]
    band_cols = winds.shape[4]
    lat_rows = winds.shape[5]
    probes = probe_sign.shape[0]
    week_count, _, own = prior_precision.shape
    sections = lax.axis_size("tm")
    bands = lax.axis_size("lon")
    hours = sections * hours_sec
    lev_pad = -(-levels // 8) * 8
    halo = -(-hours // 4) * 4
    left = hours
    window = -(-(own + 2 * hours) // 64) * 64
    lanes = window * probes

    shape = (hours_sec, sections, band_cols, lev_pad, 2 * window)
    pack = pl.pallas_call(
        functools.partial(
            window_kernel, (sections, levels, lev_pad, band_cols, lat_rows, own, left, window)
        ),
        out_shape=jax.ShapeDtypeStruct((sections, hours_sec) + shape[2:], jnp.bfloat16),
        grid=(hours_sec, sections),
        in_specs=[
            pl.BlockSpec(
                (2, 1, 1, levels, band_cols, lat_rows), lambda h, d: (0, 0, h, 0, 0, 0)
            )
        ],
        out_specs=pl.BlockSpec((1, 1) + shape[2:], lambda h, d: (d, h, 0, 0, 0)),
        scratch_shapes=[pltpu.VMEM((band_cols * lev_pad, 128), jnp.float32)]
        * (2 * window // 128),
        compiler_params=pltpu.CompilerParams(vmem_limit_bytes=62 << 20),
    )(winds)

    value = (2 * probe_sign[:, 0, 0] - 1).astype(jnp.float32) * obs_weight[0, 0][None]
    count = value.shape[1]
    week_row = jnp.pad(week_map.astype(jnp.float32), ((0, 0), (0, count - hours_sec)))
    bundle = jnp.concatenate([obs_cell[0].astype(jnp.float32), value, week_row], axis=0)
    ext_cols = band_cols + 2 * halo
    sem = pltpu.SemaphoreType.DMA
    w, obs = pl.pallas_call(
        functools.partial(spread_kernel, (sections, bands, band_cols, halo)),
        out_shape=(
            jax.ShapeDtypeStruct(
                (sections, hours_sec, ext_cols, lev_pad, 2 * window), jnp.bfloat16
            ),
            jax.ShapeDtypeStruct((sections, 3) + bundle.shape, jnp.float32),
        ),
        in_specs=[pl.BlockSpec(memory_space=pl.ANY)] * 2,
        out_specs=(pl.BlockSpec(memory_space=pl.ANY),) * 2,
        scratch_shapes=[sem((hours,))] * 8 + [sem((3 * sections,))] * 2 + [sem((2,))],
        compiler_params=pltpu.CompilerParams(collective_id=0, has_side_effects=True),
    )(pack, bundle)
    w = w.reshape((hours,) + w.shape[2:])
    weeks = obs[:, 0, 1 + probes, :hours_sec].astype(jnp.int32).reshape(hours)

    mix = jnp.pad(mixing.T, ((0, lev_pad - levels),) * 2)
    high_mix = lax.reduce_precision(mix, 8, 7)
    mix = jnp.concatenate([high_mix, mix - high_mix, high_mix], axis=1).astype(jnp.bfloat16)

    dims = (
        hours, hours_sec, halo, band_cols, levels, lev_pad, lat_rows, own, left, window, probes
    )
    estimate = pl.pallas_call(
        functools.partial(sweep_kernel, dims),
        out_shape=jax.ShapeDtypeStruct((week_count, band_cols, lanes), jnp.float32),
        grid_spec=pltpu.PrefetchScalarGridSpec(
            num_scalar_prefetch=1,
            grid=(hours,),
            in_specs=[
                pl.BlockSpec(mix.shape, lambda i, wk: (0, 0)),
                pl.BlockSpec((1,) + w.shape[1:], lambda i, wk: (hours - 1 - i, 0, 0, 0)),
                pl.BlockSpec(
                    (1,) + obs.shape[1:], lambda i, wk: ((hours - 1 - i) // hours_sec, 0, 0, 0)
                ),
            ],
            out_specs=pl.BlockSpec((week_count, band_cols, lanes), lambda i, wk: (0, 0, 0)),
            scratch_shapes=[
                pltpu.VMEM((ext_cols, lev_pad, lanes), jnp.float32),
                pltpu.VMEM((ext_cols, lev_pad, lanes), jnp.float32),
                pltpu.VMEM((week_count, band_cols, lanes), jnp.float32),
            ],
        ),
        compiler_params=pltpu.CompilerParams(vmem_limit_bytes=62 << 20),
    )(weeks, mix, w, obs)
    return (prior_precision + estimate[..., left : left + own])[None]


def solution(mesh):
    placed = (
        P(None, ("groups", "tm"), None, None, "lon", None),
        P(),
        P(("groups", "tm"), "lon", None),
        P(("groups", "tm"), "lon", None),
        P("probe", ("groups", "tm"), "lon", None),
        P(("groups", "tm"), None),
        P("groups", "lon", "tm"),
    )
    return jax.shard_map(
        on_device,
        mesh=mesh,
        in_specs=placed,
        out_specs=P("probe", "groups", "lon", "tm"),
        check_vma=False,
    )
```

```python
import functools

import jax
import jax.numpy as jnp
from jax import lax
from jax.experimental import pallas as pl
from jax.experimental.pallas import tpu as pltpu
from jax.sharding import PartitionSpec as P


def split2(x):
    high = x.astype(jnp.bfloat16)
    low = (x - high.astype(jnp.float32)).astype(jnp.bfloat16)
    return high, low


def sweep_kernel(dims, weeks_ref, mix_ref, winds_ref, obs_ref, out_ref, state, mixed, flux):
    hours, hours_sec, halo, band_cols, lev, lev_pad, lat_rows, own, left, window, probes = dims
    ext_cols = band_cols + 2 * halo
    lanes = window * probes
    step = pl.program_id(0)
    hour = hours - 1 - step
    first_row = lax.axis_index("tm") * own - left

    @pl.when(step == 0)
    def _():
        state[...] = jnp.zeros_like(state)
        mixed[...] = jnp.zeros_like(mixed)
        flux[...] = jnp.zeros_like(flux)

    count = obs_ref.shape[-1]

    def observed(piece):
        cell = obs_ref[0, piece, 0:1, :].astype(jnp.int32)
        level = cell // (band_cols * lat_rows)
        rest = cell - level * (band_cols * lat_rows)
        column = rest // lat_rows
        row = rest - column * lat_rows - first_row
        hit = lax.broadcasted_iota(jnp.int32, (window, count), 0) == row
        parts = [
            split2(jnp.where(hit, obs_ref[0, piece, 1 + p : 2 + p, :], 0.0)) for p in range(probes)
        ]
        rhs = jnp.concatenate([x[0] for x in parts] + [x[1] for x in parts], axis=0)
        return level, column, rhs

    def placed_sum(hot, rhs):
        got = lax.dot_general(
            hot.astype(jnp.float32).astype(jnp.bfloat16), rhs, (((1,), (1,)), ((), ())),
            preferred_element_type=jnp.float32,
        )
        return got[:, :lanes] + got[:, lanes:]

    week = weeks_ref[hour]

    @pl.when((lax.rem(hour, hours_sec) == 0) & (hour > 0))
    def _():
        for piece, (begin, width, shift) in enumerate(
            ((halo, band_cols, 0), (0, halo, -band_cols), (halo + band_cols, halo, band_cols))
        ):
            level, column, rhs = observed(piece)
            place = (column + halo + shift - begin) * lev_pad + level
            cols_at = max(n for n in range(1, 19) if width % n == 0)
            chunk = lax.broadcasted_iota(jnp.int32, (cols_at * lev_pad, count), 0)

            def body(i, carry):
                add = placed_sum(chunk == place - i * (cols_at * lev_pad), rhs)
                for c in range(cols_at):
                    at = begin + i * cols_at + c
                    state[at] += add[c * lev_pad : (c + 1) * lev_pad]
                return carry

            lax.fori_loop(0, width // cols_at, body, 0)

    @pl.when(hour == 0)
    def _():
        level, column, rhs = observed(0)
        high = -(-band_cols // 8) * 8
        chunk = lax.broadcasted_iota(jnp.int32, (high, count), 0)
        add = placed_sum(chunk == jnp.where(level == 0, column, -1), rhs)
        flux[week] += add[:band_cols]

    flux[week] += state[halo : halo + band_cols, 0, :]

    @pl.when(hour > 0)
    def _():
        mix = mix_ref[...]
        wide = 8
        deep = 4

        def mixing(i, carry):
            at = jnp.minimum(halo - hour + i * wide, ext_cols - wide)
            for c in range(0, wide, 2):
                x = jnp.concatenate([state[at + c], state[at + c + 1]], axis=1)
                low = x - x.astype(jnp.bfloat16).astype(jnp.float32)
                stack = jnp.concatenate([x, x, low], axis=0).astype(jnp.bfloat16)
                got = jnp.dot(mix, stack, preferred_element_type=jnp.float32)
                mixed[at + c] = got[:, :lanes]
                mixed[at + c + 1] = got[:, lanes:]
            return carry

        lax.fori_loop(0, (band_cols + 2 * hour + wide - 1) // wide, mixing, 0)

        lane = lax.broadcasted_iota(jnp.int32, (lev_pad, lanes), 1)
        first = lane < window
        grid_row = lax.rem(lane, window) + first_row
        keep = jnp.logical_and(grid_row >= 0, grid_row < lat_rows - 1)

        def advect(i, carry):
            at = jnp.minimum(halo - hour + 1 + i * deep, ext_cols - 1 - deep)
            packed = winds_ref[0, at - 1].astype(jnp.float32)
            west = jnp.where(first, packed, pltpu.roll(packed, window, 1))
            before, here = mixed[at - 1], mixed[at]
            for c in range(deep):
                after = mixed[at + c + 1]
                packed = winds_ref[0, at + c].astype(jnp.float32)
                turned = pltpu.roll(packed, window, 1)
                east = jnp.where(first, packed, turned)
                north = jnp.where(keep, jnp.where(first, turned, packed), 0.0)
                south = pltpu.roll(north, 1, 1)
                g = (
                    here
                    + jnp.maximum(east, 0.0) * (after - here)
                    + jnp.minimum(west, 0.0) * (here - before)
                )
                above = pltpu.roll(g, lanes - 1, 1)
                below = pltpu.roll(g, 1, 1)
                state[at + c] = (
                    g + jnp.maximum(north, 0.0) * (above - g) + jnp.minimum(south, 0.0) * (g - below)
                )
                before, here, west = here, after, east
            return carry

        lax.fori_loop(0, (band_cols + 2 * hour - 2 + deep - 1) // deep, advect, 0)

    @pl.when(step == hours - 1)
    def _():
        square = flux[...] * flux[...]
        rolled = [
            square[w] + pltpu.roll(square[w], lanes - window, 1) for w in range(square.shape[0])
        ]
        for w in range(square.shape[0]):
            out_ref[w] = rolled[w] * 0.5


def window_kernel(dims, winds_ref, out_ref, *tmp):
    sections, lev, lev_pad, cols, lat, own, left, window = dims
    lane = lax.broadcasted_iota(jnp.int32, (cols, 128), 1)

    @pl.when((pl.program_id(0) == 0) & (pl.program_id(1) == 0))
    def _():
        for part in tmp:
            part[...] = jnp.zeros_like(part)

    def tile(comp, i, v):
        x = winds_ref[comp, 0, 0, i, :, v * 128 : min(v * 128 + 128, lat)].astype(jnp.float32)
        if x.shape[1] < 128:
            x = jnp.concatenate([x, jnp.zeros((cols, 128 - x.shape[1]), jnp.float32)], axis=1)
        return x

    def fill(start):
        def level(i, carry):
            for n, part in enumerate(tmp):
                both = jnp.zeros((cols, 128), jnp.float32)
                for comp in range(2):
                    base = comp * window - start
                    for v in range(-(-lat // 128)):
                        low = max(comp * window, base + v * 128, n * 128)
                        high = min((comp + 1) * window, base + min(v * 128 + 128, lat), n * 128 + 128)
                        if low < high:
                            x = tile(comp, i, v)
                            if base % 128:
                                x = pltpu.roll(x, base % 128, 1)
                            inside = (lane >= low - n * 128) & (lane < high - n * 128)
                            both = jnp.where(inside, x, both)
                part[pl.ds(i, cols, stride=lev_pad), :] = both
            return carry

        lax.fori_loop(0, lev, level, 0, unroll=4)

    for d in range(sections):
        pl.when(pl.program_id(1) == d)(functools.partial(fill, d * own - left))

    def column(c, carry):
        for n, part in enumerate(tmp):
            block = part[pl.ds(pl.multiple_of(c * lev_pad, 8), lev_pad), :]
            out_ref[0, 0, c, :, n * 128 : (n + 1) * 128] = block.astype(jnp.bfloat16)
        return carry

    lax.fori_loop(0, cols, column, 0, unroll=4)


def spread_kernel(dims, pack, bundle, winds, obs, zs, zr, xs, xr, hs, hr, gs, gr, os, orr, local):
    sections, bands, cols, halo = dims
    me = lax.axis_index("tm")
    band = lax.axis_index("lon")
    core = lax.axis_index("probe")
    half = cols // 2
    sides = (band, lax.rem(band + 1, bands), lax.rem(band + bands - 1, bands))

    def remote(src, dst, send, recv, tm, lon, probe):
        copy = pltpu.make_async_remote_copy(
            src_ref=src, dst_ref=dst, send_sem=send, recv_sem=recv,
            device_id={"tm": tm, "lon": lon, "probe": probe},
            device_id_type=pl.DeviceIdType.MESH,
        )
        copy.start()
        return copy

    barrier = pltpu.get_barrier_semaphore()
    for k in range(sections):
        tm = lax.rem(me + k, sections)
        for n, lon in enumerate(sides):
            if k or n:
                pl.semaphore_signal(
                    barrier, inc=1, device_id={"tm": tm, "lon": lon, "probe": core},
                    device_id_type=pl.DeviceIdType.MESH,
                )
    pl.semaphore_signal(
        barrier, inc=1, device_id={"tm": me, "lon": band, "probe": 1 - core},
        device_id_type=pl.DeviceIdType.MESH,
    )
    own_winds = pltpu.make_async_copy(pack.at[me], winds.at[me, :, pl.ds(halo, cols)], local.at[0])
    own_winds.start()
    own_obs = pltpu.make_async_copy(bundle, obs.at[me, 0], local.at[1])
    own_obs.start()
    pl.semaphore_wait(barrier, 3 * sections)

    mine = pl.ds(halo + half * core, half)
    beside = lax.rem(band + bands + 2 * core - 1, bands)
    copies = []
    hours_sec = winds.shape[1]
    hours = range(hours_sec - 1, -1, -1)
    for h in hours:
        for k in range(1, sections):
            tm = lax.rem(me + k, sections)
            copies.append(
                remote(
                    pack.at[tm, h, pl.ds(half * core, half)], winds.at[me, h, mine],
                    zs.at[k * hours_sec + h], zr.at[me * hours_sec + h], tm, band, core,
                )
            )
    for k in range(sections):
        tm = lax.rem(me + k, sections)
        for n, lon in enumerate(sides):
            if k or n:
                copies.append(
                    remote(
                        bundle, obs.at[me, n], os.at[3 * k + n], orr.at[3 * me + n], tm, lon, core
                    )
                )
    own_winds.wait()
    own_obs.wait()

    def described(src, dst, send, recv, lon, probe):
        return pltpu.make_async_remote_copy(
            src_ref=src, dst_ref=dst, send_sem=send, recv_sem=recv,
            device_id={"tm": me, "lon": lon, "probe": probe},
            device_id_type=pl.DeviceIdType.MESH,
        )

    def z_copy(s, h):
        place = winds.at[s, h, mine]
        return described(place, place, zs.at[0], zr.at[s * hours_sec + h], beside, core)

    def h_copy(s, h):
        place = winds.at[s, h, mine]
        at = s * hours_sec + h
        return described(place, place, hs.at[at], hr.at[at], band, 1 - core)

    depths = [min(halo, (s + 1) * hours_sec) for s in range(sections)]

    def x_copy(s, h):
        depth = depths[s]
        at = s * hours_sec + h
        src = winds.at[s, h, pl.ds(halo + core * (cols - depth), depth)]
        dst = winds.at[s, h, pl.ds(halo - depth + (1 - core) * (cols + depth), depth)]
        return (
            described(src, dst, xs.at[at], xr.at[at], beside, core),
            described(dst, dst, gs.at[at], gr.at[at], band, 1 - core),
        )

    order = [(s, h) for h in hours for s in range(sections - 1, -1, -1)]
    edges = {at: x_copy(*at) for at in order}
    for at in order:

        @pl.when(me == at[0])
        def _():
            edges[at][0].start()

    for at in order:

        @pl.when(me != at[0])
        def _():
            z_copy(*at).wait_recv()
            copy = h_copy(*at)
            copy.start()
            if depths[at[0]] > half:
                copy.wait_recv()
            edges[at][0].start()

    for at in order:
        edges[at][0].wait_recv()
        edges[at][1].start()
    for at in order:

        @pl.when(me != at[0])
        def _():
            copy = h_copy(*at)
            if depths[at[0]] <= half:
                copy.wait_recv()
            copy.wait_send()

        edges[at][0].wait_send()
        edges[at][1].wait()
    for copy in copies:
        copy.wait_send()
    for k in range(sections):
        source = lax.rem(me + k, sections)
        for n in range(3):
            if k or n:
                place = obs.at[source, n]
                described(
                    place, place, os.at[0], orr.at[3 * source + n], beside, core
                ).wait_recv()


def on_device(winds, mixing, obs_cell, obs_weight, probe_sign, week_map, prior_precision):
    hours_sec = winds.shape[2]
    levels = winds.shape[3]
    band_cols = winds.shape[4]
    lat_rows = winds.shape[5]
    probes = probe_sign.shape[0]
    week_count, _, own = prior_precision.shape
    sections = lax.axis_size("tm")
    bands = lax.axis_size("lon")
    hours = sections * hours_sec
    lev_pad = -(-levels // 8) * 8
    halo = -(-hours // 4) * 4
    left = hours
    window = -(-(own + 2 * hours) // 64) * 64
    lanes = window * probes

    shape = (hours_sec, sections, band_cols, lev_pad, 2 * window)
    pack = pl.pallas_call(
        functools.partial(
            window_kernel, (sections, levels, lev_pad, band_cols, lat_rows, own, left, window)
        ),
        out_shape=jax.ShapeDtypeStruct((sections, hours_sec) + shape[2:], jnp.bfloat16),
        grid=(hours_sec, sections),
        in_specs=[
            pl.BlockSpec(
                (2, 1, 1, levels, band_cols, lat_rows), lambda h, d: (0, 0, h, 0, 0, 0)
            )
        ],
        out_specs=pl.BlockSpec((1, 1) + shape[2:], lambda h, d: (d, h, 0, 0, 0)),
        scratch_shapes=[pltpu.VMEM((band_cols * lev_pad, 128), jnp.float32)]
        * (2 * window // 128),
        compiler_params=pltpu.CompilerParams(vmem_limit_bytes=40 << 20),
    )(winds)

    value = (2 * probe_sign[:, 0, 0] - 1).astype(jnp.float32) * obs_weight[0, 0][None]
    count = value.shape[1]
    week_row = jnp.pad(week_map.astype(jnp.float32), ((0, 0), (0, count - hours_sec)))
    bundle = jnp.concatenate([obs_cell[0].astype(jnp.float32), value, week_row], axis=0)
    ext_cols = band_cols + 2 * halo
    sem = pltpu.SemaphoreType.DMA
    w, obs = pl.pallas_call(
        functools.partial(spread_kernel, (sections, bands, band_cols, halo)),
        out_shape=(
            jax.ShapeDtypeStruct(
                (sections, hours_sec, ext_cols, lev_pad, 2 * window), jnp.bfloat16
            ),
            jax.ShapeDtypeStruct((sections, 3) + bundle.shape, jnp.float32),
        ),
        in_specs=[pl.BlockSpec(memory_space=pl.ANY)] * 2,
        out_specs=(pl.BlockSpec(memory_space=pl.ANY),) * 2,
        scratch_shapes=[sem((hours,))] * 8 + [sem((3 * sections,))] * 2 + [sem((2,))],
        compiler_params=pltpu.CompilerParams(collective_id=0, has_side_effects=True),
    )(pack, bundle)
    w = w.reshape((hours,) + w.shape[2:])
    weeks = obs[:, 0, 1 + probes, :hours_sec].astype(jnp.int32).reshape(hours)

    mix = jnp.pad(mixing.T, ((0, lev_pad - levels),) * 2)
    high_mix = lax.reduce_precision(mix, 8, 7)
    mix = jnp.concatenate([high_mix, mix - high_mix, high_mix], axis=1).astype(jnp.bfloat16)

    dims = (
        hours, hours_sec, halo, band_cols, levels, lev_pad, lat_rows, own, left, window, probes
    )
    estimate = pl.pallas_call(
        functools.partial(sweep_kernel, dims),
        out_shape=jax.ShapeDtypeStruct((week_count, band_cols, lanes), jnp.float32),
        grid_spec=pltpu.PrefetchScalarGridSpec(
            num_scalar_prefetch=1,
            grid=(hours,),
            in_specs=[
                pl.BlockSpec(mix.shape, lambda i, wk: (0, 0)),
                pl.BlockSpec((1,) + w.shape[1:], lambda i, wk: (hours - 1 - i, 0, 0, 0)),
                pl.BlockSpec(
                    (1,) + obs.shape[1:], lambda i, wk: ((hours - 1 - i) // hours_sec, 0, 0, 0)
                ),
            ],
            out_specs=pl.BlockSpec((week_count, band_cols, lanes), lambda i, wk: (0, 0, 0)),
            scratch_shapes=[
                pltpu.VMEM((ext_cols, lev_pad, lanes), jnp.float32),
                pltpu.VMEM((ext_cols, lev_pad, lanes), jnp.float32),
                pltpu.VMEM((week_count, band_cols, lanes), jnp.float32),
            ],
        ),
        compiler_params=pltpu.CompilerParams(vmem_limit_bytes=62 << 20),
    )(weeks, mix, w, obs)
    return (prior_precision + estimate[..., left : left + own])[None]


def solution(mesh):
    placed = (
        P(None, ("groups", "tm"), None, None, "lon", None),
        P(),
        P(("groups", "tm"), "lon", None),
        P(("groups", "tm"), "lon", None),
        P("probe", ("groups", "tm"), "lon", None),
        P(("groups", "tm"), None),
        P("groups", "lon", "tm"),
    )
    return jax.shard_map(
        on_device,
        mesh=mesh,
        in_specs=placed,
        out_specs=P("probe", "groups", "lon", "tm"),
        check_vma=False,
    )
```
